32 devices in a mesh: dp: 4 (over y, x), dev: 8 (over z, core).
Axes of the slice: x: 2, y: 2, z: 4, core: 2. Of those that a mesh axis runs over, the one named last changes fastest.
Arguments:
- frames: bfloat16 [32, 48, 8192], P(('dp', 'dev')), parts along dimension 0, may hold values from -6 to 6
- clip_ids: int32 [32], P(('dp', 'dev')), parts along dimension 0, may hold values from 0 to 1, never falling along the last dimension, each value on 1 to 7 neighbouring positions
- norm_gain: float32 [2, 64], replicated, may hold values from 0.25 to 1.75
- space_kernel: bfloat16 [2, 3, 3, 64, 64], replicated, may hold values from -0.25 to 0.25
- time_kernel: bfloat16 [2, 5, 64, 64], replicated, may hold values from -0.3125 to 0.3125
Outputs:
- encoded: bfloat16 [32, 48, 8192], P(('dp', 'dev')), parts along dimension 0
The draws below stay inside these ranges and needn't reach their ends.
There are 4 independent parts, one for each index of `dp`. The reference program is written for one: setup_inputs(seed, part) draws one part's arguments, and reference() takes and returns one part's arrays. A program takes and returns all parts, laid end to end along the dimension named above; an argument that names none is the same for every part. Nothing has to cross between parts.
Inputs may be any that keep to these rules, and one draw needn't show every extreme that they name: `clip_ids`: clip ids never fall along the frames; each clip holds 1 to 7 frames, one exactly 7.
All inputs are finite; a program needn't handle non-finite values.
Results may differ from the reference program's by a relative error of at most 0.0061.
Values may be sent and summed in bfloat16 or wider, within the bound.
No kernel may reach another device: no remote copies, remote signals or barrier semaphores. Data moves between devices by JAX's collectives and lax.ppermute only.
A program may use at most 64 MiB of HBM per device.

```python
import math
import jax
import jax.numpy as jnp
import numpy as np
from jax import lax

C = 64
GROUPS = 32
W = 128
H = 48
TIME_TAPS = 5
TIME_DILATION = 2
BLOCKS = 2
FRAMES = 8
CLIPS = 2
CLIP_MOST = 7


def block_scale(rng, extent, pieces, least, top_value):
    loudness, own = 1.0, jax.random.fold_in(rng, 6)
    for dim, blocks in pieces:
        draws = jnp.exp(jax.random.uniform(jax.random.fold_in(own, dim), (blocks,), jnp.float32, least / len(pieces), top_value / len(pieces)))
        loudness = loudness * jnp.repeat(draws, extent[dim] // blocks).reshape([-1 if axis == dim else 1 for axis in range(len(extent))])
    return loudness


def split_up(number_of, total, reach, lean):
    portions = [(1 << 20) // math.isqrt(rank ** lean) + 1 for rank in range(2, number_of + 1)]
    spare, given = total - reach - (number_of - 1), [1] * (number_of - 1)
    while spare > 0:
        movable = [i for i in range(number_of - 1) if given[i] < reach]
        pool, left = sum([portions[i] for i in movable]), spare
        for i in movable:
            more = min(reach - given[i], max(1, left * portions[i] // pool), spare)
            given[i] = given[i] + more
            spare = spare - more
    return np.array([reach] + given)


def ragged_sizes(stream_key, amount, total, bound, slope):
    if amount == 2:
        one = jax.random.randint(stream_key, (), max(1, total - bound), min(bound, total - 1) + 1)
        return jnp.stack([one, total - one])
    lengths = jnp.asarray(split_up(amount, total, bound, slope), jnp.int32)
    couples = (amount - 1) // 2
    source_of, taker = lengths[1:1 + 2 * couples:2], lengths[2:2 + 2 * couples:2]
    margin = jnp.minimum(source_of - 1, bound - taker)
    passed = jax.random.randint(jax.random.fold_in(stream_key, 1), (couples,), 0, 1 << 20) % (margin + 1)
    lengths = lengths.at[1:1 + 2 * couples:2].set(source_of - passed).at[2:2 + 2 * couples:2].set(taker + passed)
    return lengths[jax.random.permutation(jax.random.fold_in(stream_key, 2), amount)]


def gaussian(key, dims, deviation, limit, shards=(), held_as=jnp.bfloat16):
    entries = jax.random.normal(key, dims, jnp.float32) * deviation
    if len(shards) > 0:
        entries = block_scale(key, dims, shards, -0.22, 0.18) * entries
    return jnp.clip(entries, min=-limit, max=limit).astype(held_as)


def setup_inputs(seed: int = 0, part: int = 0) -> dict:
    splits = jax.random.split(jax.random.key(seed), 6)
    part_splits = jax.random.split(jax.random.fold_in(splits[5], part), 6)
    frames = gaussian(part_splits[0], (FRAMES, H, W * C), 1.0, 6.0, ((0, 8),))
    clip_ids = jnp.searchsorted(jnp.cumsum(ragged_sizes(part_splits[1], CLIPS, FRAMES, CLIP_MOST, 2)), jnp.arange(FRAMES), side="right").astype(jnp.int32)
    norm_gain = jnp.clip(1.0 + 0.15 * jax.random.normal(splits[2], (BLOCKS, C), jnp.float32), 0.25, 1.75)
    space_kernel = gaussian(splits[3], (BLOCKS, 3, 3, C, C), (9 * C) ** -0.5, 0.25)
    time_kernel = gaussian(splits[4], (BLOCKS, TIME_TAPS, C, C), (TIME_TAPS * C) ** -0.5, 0.3125)
    return {"frames": frames, "clip_ids": clip_ids, "norm_gain": norm_gain, "space_kernel": space_kernel, "time_kernel": time_kernel}


def one_block(values, clip_ids, gain, space_w, time_w):
    frame_count = values.shape[0]
    xf = values.astype(jnp.float32).reshape(frame_count, H, W, C)
    grouped = xf.reshape(frame_count, H, W, GROUPS, C // GROUPS)
    center = lax.optimization_barrier(jnp.mean(grouped, axis=(1, 2, 4), keepdims=True))
    spread = lax.optimization_barrier(jnp.mean((grouped - center) * (grouped - center), axis=(1, 2, 4), keepdims=True))
    normal = ((grouped - center) / jnp.sqrt(spread + 1e-06)).reshape(frame_count, H, W, C)
    act = jax.nn.silu(normal * gain).astype(jnp.bfloat16)
    padded = jnp.pad(act, ((0, 0), (1, 1), (1, 1), (0, 0)))
    total = jnp.zeros((frame_count * H * W, C), jnp.float32)
    for i in range(3):
        for j in range(3):
            window = padded[:, i:i + H, j:j + W, :].reshape(-1, C)
            total = total + jnp.dot(window, space_w[i, j], preferred_element_type=jnp.float32)
    spat = total.astype(jnp.bfloat16).reshape(frame_count, H, W, C)
    index = jnp.arange(frame_count, dtype=jnp.int32)
    result = jnp.zeros((frame_count * H * W, C), jnp.float32)
    for kernel_step in range(TIME_TAPS):
        frame_offset = (kernel_step - TIME_TAPS // 2) * TIME_DILATION
        source = index + frame_offset
        inside = (source >= 0) & (source < frame_count)
        source = jnp.clip(source, 0, frame_count - 1).astype(jnp.int32)
        same = inside & (clip_ids[source] == clip_ids)
        moved = jnp.take(spat, source, axis=0) * same.astype(jnp.bfloat16)[:, None, None, None]
        result = result + jnp.dot(moved.reshape(-1, C), time_w[kernel_step], preferred_element_type=jnp.float32)
    update = lax.optimization_barrier(result.astype(jnp.bfloat16))
    summed = values.astype(jnp.float32) + update.astype(jnp.float32).reshape(values.shape)
    return summed.astype(jnp.bfloat16)

def reference(frames, clip_ids, norm_gain, space_kernel, time_kernel):
    current = frames
    for block_index in range(BLOCKS):
        current = one_block(current, clip_ids, norm_gain[block_index], space_kernel[block_index], time_kernel[block_index])
    return current
```

```python
import functools

import jax
import jax.numpy as jnp
from jax import lax
from jax.experimental import pallas as pl
from jax.experimental.pallas import tpu as pltpu
from jax.sharding import PartitionSpec as P

GROUPS = 32
TIME_TAPS = 5
TIME_DILATION = 2
BLOCKS = 2
LANES = 128
REACH = TIME_TAPS // 2

WHOLE = pl.BlockSpec(memory_space=pltpu.VMEM)
PLACED = pl.BlockSpec(memory_space=pl.ANY)
GRANT = 26 << 20


def lane_tile(index, tiles=1):
    return pl.ds(pl.multiple_of(index * LANES, LANES), tiles * LANES)


def float_tile(frame, index):
    return frame[:, lane_tile(index)].astype(jnp.float32)


def fold_groups(total, width):
    per_group = width // GROUPS
    total = jnp.broadcast_to(jnp.sum(total, axis=0, keepdims=True), total.shape)
    total = total + pltpu.roll(total, width, 1)
    lane = lax.broadcasted_iota(jnp.int32, total.shape, 1)
    step = 1
    while step < per_group:
        ahead, behind = pltpu.roll(total, LANES - step, 1), pltpu.roll(total, step, 1)
        total = total + jnp.where((lane // step) % 2 == 0, ahead, behind)
        step *= 2
    return total[:1]


def by_sublane(values):
    return jnp.sum(values.reshape(-1, 8, LANES), axis=0)


def statistics(frame, tiles, width):
    count = frame.shape[0] * tiles * LANES // GROUPS
    zero = jnp.zeros((8, LANES), jnp.float32)

    def gather(index, total):
        return total + by_sublane(float_tile(frame, index))

    mean = fold_groups(lax.fori_loop(0, tiles, gather, zero, unroll=16), width) / count

    def spread(index, total):
        shifted = float_tile(frame, index) - mean
        return total + by_sublane(shifted * shifted)

    squares = fold_groups(lax.fori_loop(0, tiles, spread, zero, unroll=16), width)
    return mean, lax.rsqrt(squares / count + 1e-06)


def activate(frame, acts, gain, tiles, width):
    mean, scale = statistics(frame, tiles, width)
    scale = scale * jnp.concatenate([gain] * (LANES // width), 1) * 0.5
    height = frame.shape[0]
    lane = lax.broadcasted_iota(jnp.int32, (height, LANES), 1)
    row = lax.broadcasted_iota(jnp.int32, (height, LANES), 0)
    above, level, below = acts

    def put(index, values):
        at = lane_tile(index)
        up, down = pltpu.roll(values, 1, 0), pltpu.roll(values, height - 1, 0)
        above[:, at] = jnp.where(row == 0, 0.0, up).astype(jnp.bfloat16)
        level[:, at] = values.astype(jnp.bfloat16)
        below[:, at] = jnp.where(row == height - 1, 0.0, down).astype(jnp.bfloat16)

    def step(index, last):
        half = (float_tile(frame, index) - mean) * scale
        turned = pltpu.roll(half + half * jnp.tanh(half), width, 1)
        put(index, jnp.where(lane < width, last, turned))
        return turned

    last = lax.fori_loop(0, tiles, step, jnp.zeros((height, LANES), jnp.float32), unroll=8)
    put(tiles, jnp.where(lane < width, last, 0.0))


def spatial(acts, bands, result, tiles):
    height = result.shape[0]
    pack = 32 if tiles % 32 == 0 else 1

    def block(first, carry):
        rows = [
            jnp.concatenate([act[:, lane_tile(first * pack + i, 2)] for act in acts], 1)
            for i in range(pack)
        ]
        total = jnp.dot(jnp.concatenate(rows, 0), bands, preferred_element_type=jnp.float32)
        total = total.astype(jnp.bfloat16)
        for i in range(pack):
            result[:, lane_tile(first * pack + i)] = total[i * height : (i + 1) * height]
        return carry

    lax.fori_loop(0, tiles // pack, block, 0)


def normed_conv(frame, acts, bands, gain, result, tiles, width):
    activate(frame, acts, gain, tiles, width)
    spatial(acts, bands, result, tiles)


def temporal(start, sources, weights, result, tiles):
    height = start.shape[0]
    pack = 32 if tiles % 32 == 0 else 1

    def block(first, carry):
        rows = [
            jnp.concatenate([source[:, lane_tile(first * pack + i)] for source in sources], 1)
            for i in range(pack)
        ]
        total = jnp.dot(jnp.concatenate(rows, 0), weights, preferred_element_type=jnp.float32)
        total = total.astype(jnp.bfloat16).astype(jnp.float32)
        for i in range(pack):
            at = lane_tile(first * pack + i)
            summed = start[:, at].astype(jnp.float32) + total[i * height : (i + 1) * height]
            result[:, at] = summed.astype(jnp.bfloat16)
        return carry

    lax.fori_loop(0, tiles // pack, block, 0)


def marked_weights(table, marks, target, places):
    rows = []
    for mark, place in zip(marks, places):
        same = (mark == target).astype(jnp.float32)
        rows.append((table[place].astype(jnp.float32) * same).astype(jnp.bfloat16))
    return jnp.concatenate(rows, 0)


def mark_of(frame, tiles):
    return frame[0:16, lane_tile(tiles)].astype(jnp.float32)[:1]


def fetch(source, target, sem):
    copy = pltpu.make_async_copy(source, target, sem)
    copy.start()
    copy.wait()


def mark_kernel(ids, frame, marked, sem):
    columns = frame.shape[-1]
    copy = pltpu.make_async_copy(frame.at[0], marked.at[:, pl.ds(0, columns)], sem)
    copy.start()
    marked[:, columns:] = jnp.full((marked.shape[0], LANES), ids[0].astype(jnp.float32)).astype(
        jnp.bfloat16
    )
    copy.wait()


def mark_frames(frames, clip_ids):
    _, height, columns = frames.shape
    return pl.pallas_call(
        mark_kernel,
        out_shape=jax.ShapeDtypeStruct((height, columns + LANES), frames.dtype),
        in_specs=[pl.BlockSpec(memory_space=pltpu.SMEM), PLACED],
        out_specs=WHOLE,
        scratch_shapes=[pltpu.SemaphoreType.DMA],
        compiler_params=pltpu.CompilerParams(vmem_limit_bytes=4 << 20),
        name="mark_frames",
    )(clip_ids, frames)


def build_bands(space, bands):
    width = space.shape[-1]
    blank = jnp.zeros((width, width), jnp.bfloat16)
    for block in range(BLOCKS):
        for r in range(3):
            for a in range(4):
                pair = [space[block, r, a - b] if 0 <= a - b <= 2 else blank for b in (0, 1)]
                bands[block, pl.ds((r * 4 + a) * width, width), :] = jnp.concatenate(pair, 1)


def build_table(time, table, near):
    width = time.shape[-1]
    blank = jnp.zeros((width, width), jnp.bfloat16)
    for block in range(BLOCKS):
        for entry in range(TIME_TAPS + 2):
            if 1 <= entry <= TIME_TAPS:
                tap = jnp.where(near, entry - 1, TIME_TAPS - entry)
                matrix = time[block, tap]
            else:
                matrix = blank
            upper = jnp.concatenate([matrix, blank], 1)
            lower = jnp.concatenate([blank, matrix], 1)
            table[block, entry] = jnp.concatenate([upper, lower], 0)


def acts_scratch(height, columns):
    return [pltpu.VMEM((height, columns + LANES), jnp.bfloat16)] * 3


def like(frame, lanes=0):
    return jax.ShapeDtypeStruct((frame.shape[0], frame.shape[1] + lanes), jnp.bfloat16)


def estimate(frames):
    return pl.CostEstimate(
        flops=frames * 1_000_000_000, bytes_accessed=frames * 4_000_000, transcendentals=0
    )


def own_kernel(dims, where, frame, gains, space, time, conv, bands, table, *acts):
    tiles, width = dims
    build_bands(space, bands)
    build_table(time, table, where[0] == 1)
    normed_conv(frame, acts, bands[0], gains[0:1], conv, tiles, width)
    conv[:, lane_tile(tiles)] = frame[:, lane_tile(tiles)]


def own_call(where, frame, gains, space, time):
    height, columns = frame.shape
    width = space.shape[-1]
    tiles = columns // LANES - 1
    return pl.pallas_call(
        functools.partial(own_kernel, (tiles, width)),
        out_shape=(
            like(frame),
            jax.ShapeDtypeStruct((BLOCKS, 12 * width, LANES), jnp.bfloat16),
            jax.ShapeDtypeStruct((BLOCKS, TIME_TAPS + 2, LANES, LANES), jnp.bfloat16),
        ),
        in_specs=[pl.BlockSpec(memory_space=pltpu.SMEM)] + [WHOLE] * 4,
        out_specs=(WHOLE,) * 3,
        scratch_shapes=acts_scratch(height, columns),
        compiler_params=pltpu.CompilerParams(vmem_limit_bytes=GRANT),
        cost_estimate=estimate(1),
        name="own",
    )(where, frame, gains, space, time)


def next_kernel(dims, where, left, right, gains, bands, xn, sn, xo, so, *rest):
    tiles, width = dims
    acts, sem = rest[:3], rest[3]
    near, middle = where[0] == 1, where[1] == 1

    def conv(result, frame):
        normed_conv(frame, acts, bands[0], gains[0:1], result, tiles, width)
        result[:, lane_tile(tiles)] = frame[:, lane_tile(tiles)]

    pl.when(near)(lambda: fetch(right, xn, sem))
    pl.when(jnp.logical_not(near))(lambda: fetch(left, xn, sem))
    conv(sn, xn)

    @pl.when(jnp.logical_not(middle))
    def _():
        so[...] = jnp.zeros(so.shape, so.dtype)

    @pl.when(middle)
    def _():
        pl.when(near)(lambda: fetch(left, xo, sem))
        pl.when(jnp.logical_not(near))(lambda: fetch(right, xo, sem))
        conv(so, xo)


def next_call(where, left, right, gains, bands):
    height, columns = left.shape
    tiles, width = columns // LANES - 1, gains.shape[-1]
    return pl.pallas_call(
        functools.partial(next_kernel, (tiles, width)),
        out_shape=(like(left),) * 4,
        in_specs=[pl.BlockSpec(memory_space=pltpu.SMEM), PLACED, PLACED, WHOLE, WHOLE],
        out_specs=(WHOLE,) * 4,
        scratch_shapes=acts_scratch(height, columns) + [pltpu.SemaphoreType.DMA],
        compiler_params=pltpu.CompilerParams(vmem_limit_bytes=GRANT),
        cost_estimate=estimate(2),
        name="next",
    )(where, left, right, gains, bands)


def places(middle, target):
    one = middle.astype(jnp.int32)
    lie = [one, one + 1, one + 2, 3 - 3 * one]
    return [at - lie[target] + REACH + 1 for at in lie]


def clamped(entries):
    return [jnp.clip(entry, 0, TIME_TAPS + 1) for entry in entries]


def after_kernel(dims, *refs):
    tiles, width = dims
    where, ends, plus, minus, gains, bands, table, xs, ss, sn, so = refs[:11]
    xa, sa, xs1, ss1 = refs[11:15]
    acts, sem = refs[15:18], refs[18]
    near, middle = where[0] == 1, where[1] == 1
    outer = jnp.logical_not(middle)

    pl.when(middle)(lambda: fetch(ends, xa, sem))
    pl.when(outer & near)(lambda: fetch(minus, xa, sem))
    pl.when(outer & jnp.logical_not(near))(lambda: fetch(plus, xa, sem))
    normed_conv(xa, acts, bands[0], gains[0:1], sa, tiles, width)
    sa[:, lane_tile(tiles)] = xa[:, lane_tile(tiles)]

    sources = (ss, sn, sa, so)
    marks = [mark_of(source, tiles) for source in sources]
    weights = marked_weights(table.at[0], marks, marks[0], clamped(places(middle, 0)))
    temporal(xs, sources, weights, xs1, tiles)
    normed_conv(xs1, acts, bands[1], gains[1:2], ss1, tiles, width)


def after_call(where, ends, plus, minus, gains, bands, table, xs, ss, sn, so):
    height, columns = xs.shape
    tiles, width = columns // LANES - 1, gains.shape[-1]
    return pl.pallas_call(
        functools.partial(after_kernel, (tiles, width)),
        out_shape=(like(xs), like(xs), like(xs, -LANES), like(xs, -LANES)),
        in_specs=[pl.BlockSpec(memory_space=pltpu.SMEM)] + [PLACED] * 3 + [WHOLE] * 7,
        out_specs=(WHOLE,) * 4,
        scratch_shapes=acts_scratch(height, columns) + [pltpu.SemaphoreType.DMA],
        compiler_params=pltpu.CompilerParams(vmem_limit_bytes=GRANT),
        cost_estimate=estimate(2),
        name="after",
    )(where, ends, plus, minus, gains, bands, table, xs, ss, sn, so)


def last_kernel(dims, *refs):
    tiles, width = dims
    where, corner, gains, bands, table, ss, sn, so_mid, sa, xn, xo, xa, xs1, ss1 = refs[:14]
    out = refs[14]
    acts = refs[15:18]
    so, x1, sn1, sa1, so1, sem = refs[18:]
    middle = where[1] == 1
    outer = jnp.logical_not(middle)

    pl.when(middle)(lambda: fetch(so_mid, so, sem))
    pl.when(outer)(lambda: fetch(corner, so, sem))
    sources = (ss, sn, sa, so)
    marks = [mark_of(source, tiles) for source in sources]

    def both(target, start, result):
        entries = clamped(places(middle, target))
        weights = marked_weights(table.at[0], marks, marks[target], entries)
        temporal(start, sources, weights, x1, tiles)
        normed_conv(x1, acts, bands[1], gains[1:2], result, tiles, width)

    both(1, xn, sn1)
    both(2, xa, sa1)

    @pl.when(outer)
    def _():
        so1[...] = jnp.zeros(so1.shape, so1.dtype)

    pl.when(middle)(lambda: both(3, xo, so1))
    weights = marked_weights(table.at[1], marks, marks[0], clamped(places(middle, 0)))
    temporal(xs1, (ss1, sn1, sa1, so1), weights, out.at[0], tiles)


def last_call(where, corner, gains, bands, table, ss, sn, so, sa, xn, xo, xa, xs1, ss1):
    height, columns = xn.shape
    tiles, width = columns // LANES - 1, gains.shape[-1]
    plain = pltpu.VMEM((height, columns - LANES), jnp.bfloat16)
    return pl.pallas_call(
        functools.partial(last_kernel, (tiles, width)),
        out_shape=jax.ShapeDtypeStruct((1, height, columns - LANES), jnp.bfloat16),
        in_specs=[pl.BlockSpec(memory_space=pltpu.SMEM), PLACED] + [WHOLE] * 12,
        out_specs=WHOLE,
        scratch_shapes=acts_scratch(height, columns)
        + [pltpu.VMEM((height, columns), jnp.bfloat16)]
        + [plain] * 4
        + [pltpu.SemaphoreType.DMA],
        compiler_params=pltpu.CompilerParams(vmem_limit_bytes=GRANT),
        cost_estimate=estimate(3),
        name="last",
    )(where, corner, gains, bands, table, ss, sn, so, sa, xn, xo, xa, xs1, ss1)


def moved(values, hops):
    pairs = [(TIME_DILATION * a + c, TIME_DILATION * b + c) for a, b in hops for c in (0, 1)]
    return lax.ppermute(values, "dev", pairs)


def on_a_line(frames, clip_ids, norm_gain, space_kernel, time_kernel):
    chip = lax.axis_index("dev") // TIME_DILATION
    near, middle = chip < 2, (chip == 1) | (chip == 2)
    where = jnp.stack([near, middle]).astype(jnp.int32)
    xs = mark_frames(frames, clip_ids)
    left = moved(xs, [(0, 1), (1, 2), (2, 3)])
    right = moved(xs, [(1, 0), (2, 1), (3, 2)])
    ends = moved(xs, [(0, 2), (3, 1)])
    ss, bands, table = own_call(where, xs, norm_gain, space_kernel, time_kernel)
    corner = moved(ss, [(0, 3), (3, 0)])
    left, _ = lax.optimization_barrier((left, ss))
    right, _ = lax.optimization_barrier((right, ss))
    plus = moved(left, [(2, 3)])
    minus = moved(right, [(1, 0)])
    xn, sn, xo, so = next_call(where, left, right, norm_gain, bands)
    xa, sa, xs1, ss1 = after_call(
        where, ends, plus, minus, norm_gain, bands, table, xs, ss, sn, so
    )
    return last_call(
        where, corner, norm_gain, bands, table, ss, sn, so, sa, xn, xo, xa, xs1, ss1
    )


def conv_kernel(dims, block, frame, gains, bands, conv, *acts):
    tiles, width = dims
    normed_conv(frame, acts, bands[block], gains[block : block + 1], conv, tiles, width)
    conv[:, lane_tile(tiles)] = frame[:, lane_tile(tiles)]


def conv_call(block, frame, gains, bands):
    height, columns = frame.shape
    tiles, width = columns // LANES - 1, gains.shape[-1]
    return pl.pallas_call(
        functools.partial(conv_kernel, (tiles, width), block),
        out_shape=like(frame),
        in_specs=[WHOLE] * 3,
        out_specs=WHOLE,
        scratch_shapes=acts_scratch(height, columns),
        compiler_params=pltpu.CompilerParams(vmem_limit_bytes=GRANT),
        name="conv",
    )(frame, gains, bands)


def mix_kernel(tiles, block, frame, table, *refs):
    sources, result = refs[:TIME_TAPS], refs[TIME_TAPS]
    marks = [mark_of(source, tiles) for source in sources]
    entries = range(1, TIME_TAPS + 1)
    weights = marked_weights(table.at[block], marks, marks[REACH], entries)
    temporal(frame, sources, weights, result, tiles)
    result[:, lane_tile(tiles)] = frame[:, lane_tile(tiles)]


def mix_call(block, frame, table, sources):
    return pl.pallas_call(
        functools.partial(mix_kernel, frame.shape[1] // LANES - 1, block),
        out_shape=like(frame),
        in_specs=[WHOLE] * (2 + TIME_TAPS),
        out_specs=WHOLE,
        compiler_params=pltpu.CompilerParams(vmem_limit_bytes=GRANT),
        name="mix",
    )(frame, table, *sources)


def by_relays(frames, clip_ids, norm_gain, space_kernel, time_kernel):
    chips = lax.axis_size("dev") // TIME_DILATION
    up = [(i, i + 1) for i in range(chips - 1)]
    down = [(i + 1, i) for i in range(chips - 1)]
    frame = mark_frames(frames, clip_ids)
    where = jnp.ones((2,), jnp.int32)
    conv, bands, table = own_call(where, frame, norm_gain, space_kernel, time_kernel)
    for block in range(BLOCKS):
        if block > 0:
            conv = conv_call(block, frame, norm_gain, bands)
        sources = [conv]
        for _ in range(REACH):
            sources = [moved(sources[0], up)] + sources + [moved(sources[-1], down)]
        frame = mix_call(block, frame, table, sources)
    return frame[None, :, : frames.shape[2]]


def per_device(*args):
    return (on_a_line if lax.axis_size("dev") == 8 else by_relays)(*args)


def solution(mesh):
    return jax.shard_map(
        per_device,
        mesh=mesh,
        in_specs=(P(("dp", "dev"), None, None), P(("dp", "dev")), P(), P(), P()),
        out_specs=P(("dp", "dev"), None, None),
        check_vma=False,
    )
```

```python
import functools

import jax
import jax.numpy as jnp
from jax import lax
from jax.experimental import pallas as pl
from jax.experimental.pallas import tpu as pltpu
from jax.sharding import PartitionSpec as P

GROUPS = 32
TIME_TAPS = 5
TIME_DILATION = 2
BLOCKS = 2
LANES = 128
REACH = TIME_TAPS // 2

WHOLE = pl.BlockSpec(memory_space=pltpu.VMEM)
PLACED = pl.BlockSpec(memory_space=pl.ANY)
GRANT = 26 << 20


def lane_tile(index, tiles=1):
    return pl.ds(pl.multiple_of(index * LANES, LANES), tiles * LANES)


def float_tile(frame, index):
    return frame[:, lane_tile(index)].astype(jnp.float32)


def fold_groups(total, width):
    per_group = width // GROUPS
    total = jnp.broadcast_to(jnp.sum(total, axis=0, keepdims=True), total.shape)
    total = total + pltpu.roll(total, width, 1)
    lane = lax.broadcasted_iota(jnp.int32, total.shape, 1)
    step = 1
    while step < per_group:
        ahead, behind = pltpu.roll(total, LANES - step, 1), pltpu.roll(total, step, 1)
        total = total + jnp.where((lane // step) % 2 == 0, ahead, behind)
        step *= 2
    return total[:1]


def by_sublane(values):
    return jnp.sum(values.reshape(-1, 8, LANES), axis=0)


def statistics(frame, tiles, width):
    share = frame.shape[0] * LANES // GROUPS
    pivot = fold_groups(by_sublane(float_tile(frame, 0)), width) / share
    zero = jnp.zeros((8, LANES), jnp.float32)

    def gather(index, totals):
        shifted = float_tile(frame, index) - pivot
        return totals[0] + by_sublane(shifted), totals[1] + by_sublane(shifted * shifted)

    sums, squares = lax.fori_loop(0, tiles, gather, (zero, zero), unroll=16)
    offset = fold_groups(sums, width) / (share * tiles)
    spread = fold_groups(squares, width) / (share * tiles) - offset * offset
    return pivot + offset, lax.rsqrt(jnp.maximum(spread, 0.0) + 1e-06)


def activate(frame, act, gain, tiles, width):
    mean, scale = statistics(frame, tiles, width)
    scale = scale * jnp.concatenate([gain] * (LANES // width), 1) * 0.5
    height = frame.shape[0]
    lane = lax.broadcasted_iota(jnp.int32, (height, LANES), 1)

    def step(index, last):
        half = (float_tile(frame, index) - mean) * scale
        turned = pltpu.roll(half + half * jnp.tanh(half), width, 1)
        act[:, lane_tile(index)] = jnp.where(lane < width, last, turned).astype(jnp.bfloat16)
        return turned

    last = lax.fori_loop(0, tiles, step, jnp.zeros((height, LANES), jnp.float32), unroll=16)
    act[:, lane_tile(tiles)] = jnp.where(lane < width, last, 0.0).astype(jnp.bfloat16)


def packed(tiles):
    return 32 if tiles % 32 == 0 else 1


def spatial(act, bands, result, tiles):
    height = result.shape[0]
    pack = packed(tiles)
    row = lax.broadcasted_iota(jnp.int32, (height, LANES), 0)

    def block(first, carry):
        rows = [act[:, lane_tile(first * pack + i, 2)] for i in range(pack)]
        total = jnp.dot(jnp.concatenate(rows, 0), bands, preferred_element_type=jnp.float32)
        for i in range(pack):
            part = total[i * height : (i + 1) * height]
            above = jnp.where(row == 0, 0.0, pltpu.roll(part[:, :LANES], 1, 0))
            below = pltpu.roll(part[:, 2 * LANES :], height - 1, 0)
            below = jnp.where(row == height - 1, 0.0, below)
            summed = above + part[:, LANES : 2 * LANES] + below
            result[:, lane_tile(first * pack + i)] = summed.astype(jnp.bfloat16)
        return carry

    lax.fori_loop(0, tiles // pack, block, 0)


def normed_conv(frame, act, bands, gain, result, tiles, width):
    activate(frame, act, gain, tiles, width)
    spatial(act, bands, result, tiles)


def temporal(sources, weights, tiles, emit):
    height = sources[0].shape[0]
    pack = packed(tiles)

    def block(first, carry):
        rows = [
            jnp.concatenate([source[:, lane_tile(first * pack + i)] for source in sources], 1)
            for i in range(pack)
        ]
        total = jnp.dot(jnp.concatenate(rows, 0), weights, preferred_element_type=jnp.float32)
        for i in range(pack):
            part = total[i * height : (i + 1) * height]
            for target in range(weights.shape[1] // LANES):
                sums = part[:, target * LANES : (target + 1) * LANES]
                emit(lane_tile(first * pack + i), target, sums)
        return carry

    lax.fori_loop(0, tiles // pack, block, 0)


def adding(starts, results):
    def emit(at, target, sums):
        update = sums.astype(jnp.bfloat16).astype(jnp.float32)
        summed = starts[target][:, at].astype(jnp.float32) + update
        results[target][:, at] = summed.astype(jnp.bfloat16)

    return emit


def marked_weights(table, marks, target, places):
    rows = []
    for mark, place in zip(marks, places):
        same = (mark == target).astype(jnp.float32)
        rows.append((table[place].astype(jnp.float32) * same).astype(jnp.bfloat16))
    return jnp.concatenate(rows, 0)


def mark_of(frame, tiles):
    return frame[0:16, lane_tile(tiles)].astype(jnp.float32)[:1]


def fetch(source, target, sem):
    copy = pltpu.make_async_copy(source, target, sem)
    copy.start()
    copy.wait()


def mark_kernel(ids, frame, marked, sem):
    columns = frame.shape[-1]
    copy = pltpu.make_async_copy(frame.at[0], marked.at[:, pl.ds(0, columns)], sem)
    copy.start()
    marked[:, columns:] = jnp.full((marked.shape[0], LANES), ids[0].astype(jnp.float32)).astype(
        jnp.bfloat16
    )
    copy.wait()


def mark_frames(frames, clip_ids):
    _, height, columns = frames.shape
    return pl.pallas_call(
        mark_kernel,
        out_shape=jax.ShapeDtypeStruct((height, columns + LANES), frames.dtype),
        in_specs=[pl.BlockSpec(memory_space=pltpu.SMEM), PLACED],
        out_specs=WHOLE,
        scratch_shapes=[pltpu.SemaphoreType.DMA],
        compiler_params=pltpu.CompilerParams(vmem_limit_bytes=4 << 20),
        name="mark_frames",
    )(clip_ids, frames)


def build_bands(space, bands):
    width = space.shape[-1]
    blank = jnp.zeros((width, width), jnp.bfloat16)
    for block in range(BLOCKS):
        for r in range(3):
            for a in range(4):
                pair = [space[block, r, a - b] if 0 <= a - b <= 2 else blank for b in (0, 1)]
                at = pl.ds(a * width, width), pl.ds(r * LANES, LANES)
                bands[(block, *at)] = jnp.concatenate(pair, 1)


def build_table(time, table, near):
    width = time.shape[-1]
    blank = jnp.zeros((width, width), jnp.bfloat16)
    for block in range(BLOCKS):
        for entry in range(TIME_TAPS + 2):
            if 1 <= entry <= TIME_TAPS:
                tap = jnp.where(near, entry - 1, TIME_TAPS - entry)
                matrix = time[block, tap]
            else:
                matrix = blank
            upper = jnp.concatenate([matrix, blank], 1)
            lower = jnp.concatenate([blank, matrix], 1)
            table[block, entry] = jnp.concatenate([upper, lower], 0)


def act_scratch(height, columns):
    return [pltpu.VMEM((height, columns), jnp.bfloat16)]


def like(frame, lanes=0):
    return jax.ShapeDtypeStruct((frame.shape[0], frame.shape[1] + lanes), jnp.bfloat16)


def estimate(frames):
    return pl.CostEstimate(
        flops=frames * 1_000_000_000, bytes_accessed=frames * 4_000_000, transcendentals=0
    )


def own_kernel(dims, where, frame, gains, space, time, conv, bands, table, act):
    tiles, width = dims
    build_bands(space, bands)
    build_table(time, table, where[0] == 1)
    normed_conv(frame, act, bands[0], gains[0:1], conv, tiles, width)
    conv[:, lane_tile(tiles)] = frame[:, lane_tile(tiles)]


def own_call(where, frame, gains, space, time):
    height, columns = frame.shape
    width = space.shape[-1]
    tiles = columns // LANES - 1
    return pl.pallas_call(
        functools.partial(own_kernel, (tiles, width)),
        out_shape=(
            like(frame),
            jax.ShapeDtypeStruct((BLOCKS, 4 * width, 3 * LANES), jnp.bfloat16),
            jax.ShapeDtypeStruct((BLOCKS, TIME_TAPS + 2, LANES, LANES), jnp.bfloat16),
        ),
        in_specs=[pl.BlockSpec(memory_space=pltpu.SMEM)] + [WHOLE] * 4,
        out_specs=(WHOLE,) * 3,
        scratch_shapes=act_scratch(height, columns),
        compiler_params=pltpu.CompilerParams(vmem_limit_bytes=GRANT),
        cost_estimate=estimate(1),
        name="own",
    )(where, frame, gains, space, time)


def next_kernel(dims, where, outer, inner, gains, bands, xn, sn, xo, so, act, sem):
    tiles, width = dims
    middle = where[1] == 1

    def conv(result, frame):
        normed_conv(frame, act, bands[0], gains[0:1], result, tiles, width)
        result[:, lane_tile(tiles)] = frame[:, lane_tile(tiles)]

    @pl.when(jnp.logical_not(middle))
    def _():
        fetch(outer, xn, sem)
        so[...] = jnp.zeros(so.shape, so.dtype)

    @pl.when(middle)
    def _():
        fetch(outer, xo, sem)
        conv(so, xo)
        fetch(inner, xn, sem)

    conv(sn, xn)


def next_call(where, outer, inner, gains, bands):
    height, columns = outer.shape
    tiles, width = columns // LANES - 1, gains.shape[-1]
    return pl.pallas_call(
        functools.partial(next_kernel, (tiles, width)),
        out_shape=(like(outer),) * 4,
        in_specs=[pl.BlockSpec(memory_space=pltpu.SMEM), PLACED, PLACED, WHOLE, WHOLE],
        out_specs=(WHOLE,) * 4,
        scratch_shapes=act_scratch(height, columns) + [pltpu.SemaphoreType.DMA],
        compiler_params=pltpu.CompilerParams(vmem_limit_bytes=GRANT),
        cost_estimate=estimate(2),
        name="next",
    )(where, outer, inner, gains, bands)


def places(middle, target):
    one = middle.astype(jnp.int32)
    lie = [one, one + 1, one + 2, 3 - 3 * one]
    return [at - lie[target] + REACH + 1 for at in lie]


def clamped(entries):
    return [jnp.clip(entry, 0, TIME_TAPS + 1) for entry in entries]


def weights_of(table, sources, middle, tiles, targets, kept):
    marks = [mark_of(source, tiles) for source in sources]

    def column(target):
        entries = clamped(places(middle, target))
        chosen = [marks[place] for place in kept], [entries[place] for place in kept]
        return marked_weights(table, chosen[0], marks[target], chosen[1])

    return jnp.concatenate([column(target) for target in targets], 1)


def after_kernel(dims, *refs):
    tiles, width = dims
    where, xa, gains, bands, table, xs, ss, sn, xo, so = refs[:10]
    sa, xs1, sums = refs[10:13]
    act, x1, ss1, so1 = refs[13:]
    middle = where[1] == 1

    normed_conv(xa, act, bands[0], gains[0:1], sa, tiles, width)
    sa[:, lane_tile(tiles)] = xa[:, lane_tile(tiles)]

    sources = (ss, sn, sa, so)
    weights = weights_of(table.at[0], sources, middle, tiles, (0, 3), (0, 1, 2, 3))
    temporal(sources, weights, tiles, adding((xs, xo), (xs1, x1)))
    normed_conv(xs1, act, bands[1], gains[1:2], ss1, tiles, width)

    @pl.when(jnp.logical_not(middle))
    def _():
        so1[...] = jnp.zeros(so1.shape, so1.dtype)

    pl.when(middle)(lambda: normed_conv(x1, act, bands[1], gains[1:2], so1, tiles, width))

    def keep(at, target, total):
        sums[:, at] = total

    weights = weights_of(table.at[1], sources, middle, tiles, (0,), (0, 3))
    temporal((ss1, so1), weights, tiles, keep)


def after_call(where, xa, gains, bands, table, xs, ss, sn, xo, so):
    height, columns = xs.shape
    tiles, width = columns // LANES - 1, gains.shape[-1]
    plain = pltpu.VMEM((height, columns - LANES), jnp.bfloat16)
    return pl.pallas_call(
        functools.partial(after_kernel, (tiles, width)),
        out_shape=(
            like(xs),
            like(xs, -LANES),
            jax.ShapeDtypeStruct((height, columns - LANES), jnp.float32),
        ),
        in_specs=[pl.BlockSpec(memory_space=pltpu.SMEM)] + [WHOLE] * 9,
        out_specs=(WHOLE,) * 3,
        scratch_shapes=act_scratch(height, columns) + [plain] * 3,
        compiler_params=pltpu.CompilerParams(vmem_limit_bytes=GRANT),
        cost_estimate=estimate(2),
        name="after",
    )(where, xa, gains, bands, table, xs, ss, sn, xo, so)


def last_kernel(dims, *refs):
    tiles, width = dims
    where, corner, gains, bands, table, ss, sn, so_mid, sa, xn, xa, xs1, sums = refs[:13]
    out = refs[13]
    act, so, xn1, xa1, sn1, sa1, sem = refs[14:]
    middle = where[1] == 1

    pl.when(middle)(lambda: fetch(so_mid, so, sem))
    pl.when(jnp.logical_not(middle))(lambda: fetch(corner, so, sem))
    sources = (ss, sn, sa, so)
    weights = weights_of(table.at[0], sources, middle, tiles, (1, 2), (0, 1, 2, 3))
    temporal(sources, weights, tiles, adding((xn, xa), (xn1, xa1)))
    normed_conv(xn1, act, bands[1], gains[1:2], sn1, tiles, width)
    normed_conv(xa1, act, bands[1], gains[1:2], sa1, tiles, width)

    def finish(at, target, total):
        update = (sums[:, at] + total).astype(jnp.bfloat16).astype(jnp.float32)
        out[0, :, at] = (xs1[:, at].astype(jnp.float32) + update).astype(jnp.bfloat16)

    weights = weights_of(table.at[1], sources, middle, tiles, (0,), (1, 2))
    temporal((sn1, sa1), weights, tiles, finish)


def last_call(where, corner, gains, bands, table, ss, sn, so, sa, xn, xa, xs1, sums):
    height, columns = xn.shape
    tiles, width = columns // LANES - 1, gains.shape[-1]
    plain = pltpu.VMEM((height, columns - LANES), jnp.bfloat16)
    return pl.pallas_call(
        functools.partial(last_kernel, (tiles, width)),
        out_shape=jax.ShapeDtypeStruct((1, height, columns - LANES), jnp.bfloat16),
        in_specs=[pl.BlockSpec(memory_space=pltpu.SMEM), PLACED] + [WHOLE] * 11,
        out_specs=WHOLE,
        scratch_shapes=act_scratch(height, columns)
        + [pltpu.VMEM((height, columns), jnp.bfloat16)]
        + [plain] * 4
        + [pltpu.SemaphoreType.DMA],
        compiler_params=pltpu.CompilerParams(vmem_limit_bytes=GRANT),
        cost_estimate=estimate(3),
        name="last",
    )(where, corner, gains, bands, table, ss, sn, so, sa, xn, xa, xs1, sums)


def moved(values, hops):
    pairs = [(TIME_DILATION * a + c, TIME_DILATION * b + c) for a, b in hops for c in (0, 1)]
    return lax.ppermute(values, "dev", pairs)


def on_a_line(frames, clip_ids, norm_gain, space_kernel, time_kernel):
    chip = lax.axis_index("dev") // TIME_DILATION
    near, middle = chip < 2, (chip == 1) | (chip == 2)
    where = jnp.stack([near, middle]).astype(jnp.int32)
    xs = mark_frames(frames, clip_ids)
    outer = moved(xs, [(0, 1), (1, 0), (2, 3), (3, 2)])
    inner = moved(xs, [(0, 0), (1, 2), (2, 1), (3, 3)])
    ss, bands, table = own_call(where, xs, norm_gain, space_kernel, time_kernel)
    outer, _ = lax.optimization_barrier((outer, ss))
    inner, _ = lax.optimization_barrier((inner, outer))
    after = moved(inner, [(0, 2), (1, 0), (2, 3), (3, 1)])
    xn, sn, xo, so = next_call(where, outer, inner, norm_gain, bands)
    sent, _ = lax.optimization_barrier((ss, sn))
    corner = moved(sent, [(0, 3), (1, 1), (2, 2), (3, 0)])
    sa, xs1, sums = after_call(where, after, norm_gain, bands, table, xs, ss, sn, xo, so)
    return last_call(where, corner, norm_gain, bands, table, ss, sn, so, sa, xn, after, xs1, sums)


def conv_kernel(dims, block, frame, gains, bands, conv, act):
    tiles, width = dims
    normed_conv(frame, act, bands[block], gains[block : block + 1], conv, tiles, width)
    conv[:, lane_tile(tiles)] = frame[:, lane_tile(tiles)]


def conv_call(block, frame, gains, bands):
    height, columns = frame.shape
    tiles, width = columns // LANES - 1, gains.shape[-1]
    return pl.pallas_call(
        functools.partial(conv_kernel, (tiles, width), block),
        out_shape=like(frame),
        in_specs=[WHOLE] * 3,
        out_specs=WHOLE,
        scratch_shapes=act_scratch(height, columns),
        compiler_params=pltpu.CompilerParams(vmem_limit_bytes=GRANT),
        name="conv",
    )(frame, gains, bands)


def mix_kernel(tiles, block, frame, table, *refs):
    sources, result = refs[:TIME_TAPS], refs[TIME_TAPS]
    marks = [mark_of(source, tiles) for source in sources]
    entries = range(1, TIME_TAPS + 1)
    weights = marked_weights(table.at[block], marks, marks[REACH], entries)
    temporal(sources, weights, tiles, adding([frame], [result]))
    result[:, lane_tile(tiles)] = frame[:, lane_tile(tiles)]


def mix_call(block, frame, table, sources):
    return pl.pallas_call(
        functools.partial(mix_kernel, frame.shape[1] // LANES - 1, block),
        out_shape=like(frame),
        in_specs=[WHOLE] * (2 + TIME_TAPS),
        out_specs=WHOLE,
        compiler_params=pltpu.CompilerParams(vmem_limit_bytes=GRANT),
        name="mix",
    )(frame, table, *sources)


def by_relays(frames, clip_ids, norm_gain, space_kernel, time_kernel):
    chips = lax.axis_size("dev") // TIME_DILATION
    up = [(i, i + 1) for i in range(chips - 1)]
    down = [(i + 1, i) for i in range(chips - 1)]
    frame = mark_frames(frames, clip_ids)
    where = jnp.ones((2,), jnp.int32)
    conv, bands, table = own_call(where, frame, norm_gain, space_kernel, time_kernel)
    for block in range(BLOCKS):
        if block > 0:
            conv = conv_call(block, frame, norm_gain, bands)
        sources = [conv]
        for _ in range(REACH):
            sources = [moved(sources[0], up)] + sources + [moved(sources[-1], down)]
        frame = mix_call(block, frame, table, sources)
    return frame[None, :, : frames.shape[2]]


def per_device(*args):
    return (on_a_line if lax.axis_size("dev") == 8 else by_relays)(*args)


def solution(mesh):
    return jax.shard_map(
        per_device,
        mesh=mesh,
        in_specs=(P(("dp", "dev"), None, None), P(("dp", "dev")), P(), P(), P()),
        out_specs=P(("dp", "dev"), None, None),
        check_vma=False,
    )
```

```python
import functools

import jax
import jax.numpy as jnp
from jax import lax
from jax.experimental import pallas as pl
from jax.experimental.pallas import tpu as pltpu
from jax.sharding import PartitionSpec as P

GROUPS = 32
TIME_TAPS = 5
TIME_DILATION = 2
BLOCKS = 2
LANES = 128
REACH = TIME_TAPS // 2

WHOLE = pl.BlockSpec(memory_space=pltpu.VMEM)
PLACED = pl.BlockSpec(memory_space=pl.ANY)
GRANT = 26 << 20


def lane_tile(index, tiles=1):
    return pl.ds(pl.multiple_of(index * LANES, LANES), tiles * LANES)


def float_tile(frame, index):
    return frame[:, lane_tile(index)].astype(jnp.float32)


def fold_groups(total, width):
    per_group = width // GROUPS
    total = jnp.broadcast_to(jnp.sum(total, axis=0, keepdims=True), total.shape)
    total = total + pltpu.roll(total, width, 1)
    lane = lax.broadcasted_iota(jnp.int32, total.shape, 1)
    step = 1
    while step < per_group:
        ahead, behind = pltpu.roll(total, LANES - step, 1), pltpu.roll(total, step, 1)
        total = total + jnp.where((lane // step) % 2 == 0, ahead, behind)
        step *= 2
    return total[:1]


def by_sublane(values):
    return jnp.sum(values.reshape(-1, 8, LANES), axis=0)


def statistics(frame, tiles, width):
    share = frame.shape[0] * LANES // GROUPS
    pivot = fold_groups(by_sublane(float_tile(frame, 0)), width) / share
    zero = jnp.zeros((8, LANES), jnp.float32)

    def gather(index, totals):
        shifted = float_tile(frame, index) - pivot
        return totals[0] + by_sublane(shifted), totals[1] + by_sublane(shifted * shifted)

    sums, squares = lax.fori_loop(0, tiles, gather, (zero, zero), unroll=16)
    offset = fold_groups(sums, width) / (share * tiles)
    spread = fold_groups(squares, width) / (share * tiles) - offset * offset
    return pivot + offset, lax.rsqrt(jnp.maximum(spread, 0.0) + 1e-06)


def activate(frame, act, gain, tiles, width):
    mean, scale = statistics(frame, tiles, width)
    scale = scale * jnp.concatenate([gain] * (LANES // width), 1) * 0.5
    height = frame.shape[0]
    lane = lax.broadcasted_iota(jnp.int32, (height, LANES), 1)

    def step(index, last):
        half = (float_tile(frame, index) - mean) * scale
        turned = pltpu.roll(half + half * jnp.tanh(half), width, 1)
        act[:, lane_tile(index)] = jnp.where(lane < width, last, turned).astype(jnp.bfloat16)
        return turned

    last = lax.fori_loop(0, tiles, step, jnp.zeros((height, LANES), jnp.float32), unroll=16)
    act[:, lane_tile(tiles)] = jnp.where(lane < width, last, 0.0).astype(jnp.bfloat16)


def packed(tiles):
    return 32 if tiles % 32 == 0 else 1


def spatial(act, bands, result, tiles):
    height = result.shape[0]
    pack = packed(tiles)
    row = lax.broadcasted_iota(jnp.int32, (height, LANES), 0)

    def block(first, carry):
        rows = [act[:, lane_tile(first * pack + i, 2)] for i in range(pack)]
        total = jnp.dot(jnp.concatenate(rows, 0), bands, preferred_element_type=jnp.float32)
        for i in range(pack):
            part = total[i * height : (i + 1) * height]
            above = jnp.where(row == 0, 0.0, pltpu.roll(part[:, :LANES], 1, 0))
            below = pltpu.roll(part[:, 2 * LANES :], height - 1, 0)
            below = jnp.where(row == height - 1, 0.0, below)
            summed = above + part[:, LANES : 2 * LANES] + below
            result[:, lane_tile(first * pack + i)] = summed.astype(jnp.bfloat16)
        return carry

    lax.fori_loop(0, tiles // pack, block, 0)


def normed_conv(frame, act, bands, gain, result, tiles, width):
    activate(frame, act, gain, tiles, width)
    spatial(act, bands, result, tiles)


def temporal(sources, weights, tiles, emit):
    height = sources[0].shape[0]
    pack = packed(tiles)

    def block(first, carry):
        rows = [
            jnp.concatenate([source[:, lane_tile(first * pack + i)] for source in sources], 1)
            for i in range(pack)
        ]
        total = jnp.dot(jnp.concatenate(rows, 0), weights, preferred_element_type=jnp.float32)
        for i in range(pack):
            part = total[i * height : (i + 1) * height]
            for target in range(weights.shape[1] // LANES):
                sums = part[:, target * LANES : (target + 1) * LANES]
                emit(lane_tile(first * pack + i), target, sums)
        return carry

    lax.fori_loop(0, tiles // pack, block, 0)


def adding(starts, results):
    def emit(at, target, sums):
        update = sums.astype(jnp.bfloat16).astype(jnp.float32)
        summed = starts[target][:, at].astype(jnp.float32) + update
        results[target][:, at] = summed.astype(jnp.bfloat16)

    return emit


def marked_weights(table, marks, target, places):
    rows = []
    for mark, place in zip(marks, places):
        same = (mark == target).astype(jnp.float32)
        rows.append((table[place].astype(jnp.float32) * same).astype(jnp.bfloat16))
    return jnp.concatenate(rows, 0)


def mark_of(frame, tiles):
    return frame[0:16, lane_tile(tiles)].astype(jnp.float32)[:1]


def fetch(source, target, sem):
    copy = pltpu.make_async_copy(source, target, sem)
    copy.start()
    copy.wait()


def mark_kernel(ids, frame, marked, sem):
    columns = frame.shape[-1]
    copy = pltpu.make_async_copy(frame.at[0], marked.at[:, pl.ds(0, columns)], sem)
    copy.start()
    marked[:, columns:] = jnp.full((marked.shape[0], LANES), ids[0].astype(jnp.float32)).astype(
        jnp.bfloat16
    )
    copy.wait()


def mark_frames(frames, clip_ids):
    _, height, columns = frames.shape
    return pl.pallas_call(
        mark_kernel,
        out_shape=jax.ShapeDtypeStruct((height, columns + LANES), frames.dtype),
        in_specs=[pl.BlockSpec(memory_space=pltpu.SMEM), PLACED],
        out_specs=WHOLE,
        scratch_shapes=[pltpu.SemaphoreType.DMA],
        compiler_params=pltpu.CompilerParams(vmem_limit_bytes=4 << 20),
        name="mark_frames",
    )(clip_ids, frames)


def build_bands(space, bands):
    width = space.shape[-1]
    blank = jnp.zeros((width, width), jnp.bfloat16)
    for block in range(BLOCKS):
        for r in range(3):
            for a in range(4):
                pair = [space[block, r, a - b] if 0 <= a - b <= 2 else blank for b in (0, 1)]
                at = pl.ds(a * width, width), pl.ds(r * LANES, LANES)
                bands[(block, *at)] = jnp.concatenate(pair, 1)


def build_table(time, table, near):
    width = time.shape[-1]
    blank = jnp.zeros((width, width), jnp.bfloat16)
    for block in range(BLOCKS):
        for entry in range(TIME_TAPS + 2):
            if 1 <= entry <= TIME_TAPS:
                tap = jnp.where(near, entry - 1, TIME_TAPS - entry)
                matrix = time[block, tap]
            else:
                matrix = blank
            upper = jnp.concatenate([matrix, blank], 1)
            lower = jnp.concatenate([blank, matrix], 1)
            table[block, entry] = jnp.concatenate([upper, lower], 0)


def act_scratch(height, columns):
    return [pltpu.VMEM((height, columns), jnp.bfloat16)]


def like(frame, lanes=0):
    return jax.ShapeDtypeStruct((frame.shape[0], frame.shape[1] + lanes), jnp.bfloat16)


def estimate(frames):
    return pl.CostEstimate(
        flops=frames * 1_000_000_000, bytes_accessed=frames * 4_000_000, transcendentals=0
    )


def own_kernel(dims, where, frame, gains, space, time, conv, given, bands, table, act):
    tiles, width = dims
    build_bands(space, bands)
    build_table(time, table, where[0] == 1)
    normed_conv(frame, act, bands[0], gains[0:1], conv, tiles, width)
    core = jnp.full((conv.shape[0] - 16, LANES), where[2].astype(jnp.float32))
    mark = jnp.concatenate([frame[0:16, lane_tile(tiles)], core.astype(jnp.bfloat16)], 0)
    conv[:, lane_tile(tiles)] = mark
    for index in range(tiles // 2):
        given[:, lane_tile(index)] = conv[:, lane_tile((1 - where[2]) * (tiles // 2) + index)]
    given[:, lane_tile(tiles // 2)] = mark


def own_call(where, frame, gains, space, time):
    height, columns = frame.shape
    width = space.shape[-1]
    tiles = columns // LANES - 1
    return pl.pallas_call(
        functools.partial(own_kernel, (tiles, width)),
        out_shape=(
            like(frame),
            like(frame, -(tiles // 2) * LANES),
            jax.ShapeDtypeStruct((BLOCKS, 4 * width, 3 * LANES), jnp.bfloat16),
            jax.ShapeDtypeStruct((BLOCKS, TIME_TAPS + 2, LANES, LANES), jnp.bfloat16),
        ),
        in_specs=[pl.BlockSpec(memory_space=pltpu.SMEM)] + [WHOLE] * 4,
        out_specs=(WHOLE,) * 4,
        scratch_shapes=act_scratch(height, columns),
        compiler_params=pltpu.CompilerParams(vmem_limit_bytes=GRANT),
        cost_estimate=estimate(1),
        name="own",
    )(where, frame, gains, space, time)


def next_kernel(dims, *refs):
    tiles, width = dims
    where, outer, inner, gains, bands, ss, given, xn, sn, xo, so, half, act, sem = refs
    middle = where[1] == 1

    def conv(result, frame):
        normed_conv(frame, act, bands[0], gains[0:1], result, tiles, width)
        result[:, lane_tile(tiles)] = frame[:, lane_tile(tiles)]

    @pl.when(jnp.logical_not(middle))
    def _():
        fetch(outer, xn, sem)
        so[...] = jnp.zeros(so.shape, so.dtype)
        near, core = where[0].astype(jnp.float32), where[2].astype(jnp.float32)
        differ = (mark_of(ss, tiles) != mark_of(given, tiles // 2)).astype(jnp.float32)
        line = differ * near + (1.0 - differ) * (1.0 - near)
        mine = jnp.broadcast_to(line, (ss.shape[0], LANES)) == core
        for index in range(tiles // 2 + 1):
            place = where[2] * (tiles // 2) + index if index < tiles // 2 else tiles
            kept = jnp.where(mine, float_tile(ss, place), float_tile(given, index))
            half[:, lane_tile(index)] = kept.astype(jnp.bfloat16)

    @pl.when(middle)
    def _():
        fetch(outer, xo, sem)
        conv(so, xo)
        fetch(inner, xn, sem)

    conv(sn, xn)


def next_call(where, outer, inner, gains, bands, ss, given):
    height, columns = outer.shape
    tiles, width = columns // LANES - 1, gains.shape[-1]
    return pl.pallas_call(
        functools.partial(next_kernel, (tiles, width)),
        out_shape=(like(outer),) * 4 + (like(given),),
        in_specs=[pl.BlockSpec(memory_space=pltpu.SMEM), PLACED, PLACED] + [WHOLE] * 4,
        out_specs=(WHOLE,) * 5,
        scratch_shapes=act_scratch(height, columns) + [pltpu.SemaphoreType.DMA],
        compiler_params=pltpu.CompilerParams(vmem_limit_bytes=GRANT),
        cost_estimate=estimate(2),
        name="next",
    )(where, outer, inner, gains, bands, ss, given)


def places(middle, target):
    one = middle.astype(jnp.int32)
    lie = [one, one + 1, one + 2, 3 - 3 * one]
    return [at - lie[target] + REACH + 1 for at in lie]


def clamped(entries):
    return [jnp.clip(entry, 0, TIME_TAPS + 1) for entry in entries]


def weights_of(table, marks, middle, targets, kept):
    def column(target):
        entries = clamped(places(middle, target))
        chosen = [marks[place] for place in kept], [entries[place] for place in kept]
        return marked_weights(table, chosen[0], marks[target], chosen[1])

    return jnp.concatenate([column(target) for target in targets], 1)


def after_kernel(dims, *refs):
    tiles, width = dims
    where, xa, gains, bands, table, xs, ss, sn, xo, so = refs[:10]
    sa, xs1, sums = refs[10:13]
    act, x1, ss1, so1 = refs[13:]
    middle = where[1] == 1

    normed_conv(xa, act, bands[0], gains[0:1], sa, tiles, width)
    sa[:, lane_tile(tiles)] = xa[:, lane_tile(tiles)]

    sources = (ss, sn, sa, so)
    marks = [mark_of(source, tiles) for source in sources]
    weights = weights_of(table.at[0], marks, middle, (0, 3), (0, 1, 2, 3))
    temporal(sources, weights, tiles, adding((xs, xo), (xs1, x1)))
    normed_conv(xs1, act, bands[1], gains[1:2], ss1, tiles, width)

    @pl.when(jnp.logical_not(middle))
    def _():
        so1[...] = jnp.zeros(so1.shape, so1.dtype)

    pl.when(middle)(lambda: normed_conv(x1, act, bands[1], gains[1:2], so1, tiles, width))

    def keep(at, target, total):
        sums[:, at] = total

    weights = weights_of(table.at[1], marks, middle, (0,), (0, 3))
    temporal((ss1, so1), weights, tiles, keep)


def after_call(where, xa, gains, bands, table, xs, ss, sn, xo, so):
    height, columns = xs.shape
    tiles, width = columns // LANES - 1, gains.shape[-1]
    plain = pltpu.VMEM((height, columns - LANES), jnp.bfloat16)
    return pl.pallas_call(
        functools.partial(after_kernel, (tiles, width)),
        out_shape=(
            like(xs),
            like(xs, -LANES),
            jax.ShapeDtypeStruct((height, columns - LANES), jnp.float32),
        ),
        in_specs=[pl.BlockSpec(memory_space=pltpu.SMEM)] + [WHOLE] * 9,
        out_specs=(WHOLE,) * 3,
        scratch_shapes=act_scratch(height, columns) + [plain] * 3,
        compiler_params=pltpu.CompilerParams(vmem_limit_bytes=GRANT),
        cost_estimate=estimate(2),
        name="after",
    )(where, xa, gains, bands, table, xs, ss, sn, xo, so)


def last_kernel(dims, *refs):
    tiles, width = dims
    where, mine, given, gains, bands, table, ss, sn, so_mid, sa, xn, xa, xs1, sums = refs[:14]
    out = refs[14]
    act, so, xn1, xa1, sn1, sa1, sem = refs[15:]
    middle = where[1] == 1

    pl.when(middle)(lambda: fetch(so_mid, so, sem.at[0]))

    @pl.when(jnp.logical_not(middle))
    def _():
        part = tiles // 2
        copies = [
            (mine.at[:, lane_tile(0, part)], so.at[:, lane_tile(where[2] * part, part)]),
            (given.at[:, lane_tile(0, part)], so.at[:, lane_tile((1 - where[2]) * part, part)]),
            (mine.at[:, lane_tile(part)], so.at[:, lane_tile(tiles)]),
        ]
        copies = [pltpu.make_async_copy(*ends, sem.at[i]) for i, ends in enumerate(copies)]
        for copy in copies:
            copy.start()
        for copy in copies:
            copy.wait()

    sources = (ss, sn, sa, so)
    marks = [mark_of(source, tiles) for source in sources]
    core = so[16:32, lane_tile(tiles)].astype(jnp.float32)[:1]
    valid = jnp.logical_or(core == where[2].astype(jnp.float32), middle)
    marks[3] = jnp.where(valid, marks[3], -1.0)
    weights = weights_of(table.at[0], marks, middle, (1, 2), (0, 1, 2, 3))
    temporal(sources, weights, tiles, adding((xn, xa), (xn1, xa1)))
    normed_conv(xn1, act, bands[1], gains[1:2], sn1, tiles, width)
    normed_conv(xa1, act, bands[1], gains[1:2], sa1, tiles, width)

    def finish(at, target, total):
        update = (sums[:, at] + total).astype(jnp.bfloat16).astype(jnp.float32)
        out[0, :, at] = (xs1[:, at].astype(jnp.float32) + update).astype(jnp.bfloat16)

    weights = weights_of(table.at[1], marks, middle, (0,), (1, 2))
    temporal((sn1, sa1), weights, tiles, finish)


def last_call(where, mine, given, gains, bands, table, ss, sn, so, sa, xn, xa, xs1, sums):
    height, columns = xn.shape
    tiles, width = columns // LANES - 1, gains.shape[-1]
    plain = pltpu.VMEM((height, columns - LANES), jnp.bfloat16)
    return pl.pallas_call(
        functools.partial(last_kernel, (tiles, width)),
        out_shape=jax.ShapeDtypeStruct((1, height, columns - LANES), jnp.bfloat16),
        in_specs=[pl.BlockSpec(memory_space=pltpu.SMEM)] + [PLACED] * 2 + [WHOLE] * 11,
        out_specs=WHOLE,
        scratch_shapes=act_scratch(height, columns)
        + [pltpu.VMEM((height, columns), jnp.bfloat16)]
        + [plain] * 4
        + [pltpu.SemaphoreType.DMA((3,))],
        compiler_params=pltpu.CompilerParams(vmem_limit_bytes=GRANT),
        cost_estimate=estimate(3),
        name="last",
    )(where, mine, given, gains, bands, table, ss, sn, so, sa, xn, xa, xs1, sums)


def moved(values, hops, swap=()):
    pairs = []
    for a, b in hops:
        for core in range(TIME_DILATION):
            target = TIME_DILATION - 1 - core if a in swap else core
            pairs.append((TIME_DILATION * a + core, TIME_DILATION * b + target))
    return lax.ppermute(values, "dev", pairs)


def on_a_line(frames, clip_ids, norm_gain, space_kernel, time_kernel):
    device = lax.axis_index("dev")
    chip = device // TIME_DILATION
    near, middle = chip < 2, (chip == 1) | (chip == 2)
    where = jnp.stack([near, middle, device % TIME_DILATION == 1]).astype(jnp.int32)
    xs = mark_frames(frames, clip_ids)
    outer = moved(xs, [(0, 1), (1, 0), (2, 3), (3, 2)])
    inner = moved(xs, [(0, 0), (1, 2), (2, 1), (3, 3)])
    ss, given, bands, table = own_call(where, xs, norm_gain, space_kernel, time_kernel)
    given = moved(given, [(chip, chip) for chip in range(4)], swap=range(4))
    outer, _ = lax.optimization_barrier((outer, given))
    inner, _ = lax.optimization_barrier((inner, outer))
    after = moved(inner, [(0, 2), (1, 0), (2, 3), (3, 1)])
    xn, sn, xo, so, half = next_call(where, outer, inner, norm_gain, bands, ss, given)
    mine = moved(half, [(0, 3), (1, 1), (2, 2), (3, 0)])
    sa, xs1, sums = after_call(where, after, norm_gain, bands, table, xs, ss, sn, xo, so)
    mine, _ = lax.optimization_barrier((mine, sums))
    given = moved(mine, [(chip, chip) for chip in range(4)], swap=(0, 3))
    return last_call(
        where, mine, given, norm_gain, bands, table, ss, sn, so, sa, xn, after, xs1, sums
    )


def conv_kernel(dims, block, frame, gains, bands, conv, act):
    tiles, width = dims
    normed_conv(frame, act, bands[block], gains[block : block + 1], conv, tiles, width)
    conv[:, lane_tile(tiles)] = frame[:, lane_tile(tiles)]


def conv_call(block, frame, gains, bands):
    height, columns = frame.shape
    tiles, width = columns // LANES - 1, gains.shape[-1]
    return pl.pallas_call(
        functools.partial(conv_kernel, (tiles, width), block),
        out_shape=like(frame),
        in_specs=[WHOLE] * 3,
        out_specs=WHOLE,
        scratch_shapes=act_scratch(height, columns),
        compiler_params=pltpu.CompilerParams(vmem_limit_bytes=GRANT),
        name="conv",
    )(frame, gains, bands)


def mix_kernel(tiles, block, frame, table, *refs):
    sources, result = refs[:TIME_TAPS], refs[TIME_TAPS]
    marks = [mark_of(source, tiles) for source in sources]
    entries = range(1, TIME_TAPS + 1)
    weights = marked_weights(table.at[block], marks, marks[REACH], entries)
    temporal(sources, weights, tiles, adding([frame], [result]))
    result[:, lane_tile(tiles)] = frame[:, lane_tile(tiles)]


def mix_call(block, frame, table, sources):
    return pl.pallas_call(
        functools.partial(mix_kernel, frame.shape[1] // LANES - 1, block),
        out_shape=like(frame),
        in_specs=[WHOLE] * (2 + TIME_TAPS),
        out_specs=WHOLE,
        compiler_params=pltpu.CompilerParams(vmem_limit_bytes=GRANT),
        name="mix",
    )(frame, table, *sources)


def by_relays(frames, clip_ids, norm_gain, space_kernel, time_kernel):
    chips = lax.axis_size("dev") // TIME_DILATION
    up = [(i, i + 1) for i in range(chips - 1)]
    down = [(i + 1, i) for i in range(chips - 1)]
    frame = mark_frames(frames, clip_ids)
    where = jnp.array([1, 0, 0], jnp.int32)
    conv, _, bands, table = own_call(where, frame, norm_gain, space_kernel, time_kernel)
    for block in range(BLOCKS):
        if block > 0:
            conv = conv_call(block, frame, norm_gain, bands)
        sources = [conv]
        for _ in range(REACH):
            sources = [moved(sources[0], up)] + sources + [moved(sources[-1], down)]
        frame = mix_call(block, frame, table, sources)
    return frame[None, :, : frames.shape[2]]


def per_device(*args):
    return (on_a_line if lax.axis_size("dev") == 8 else by_relays)(*args)


def solution(mesh):
    return jax.shard_map(
        per_device,
        mesh=mesh,
        in_specs=(P(("dp", "dev"), None, None), P(("dp", "dev")), P(), P(), P()),
        out_specs=P(("dp", "dev"), None, None),
        check_vma=False,
    )
```

```python
import functools

import jax
import jax.numpy as jnp
from jax import lax
from jax.experimental import pallas as pl
from jax.experimental.pallas import tpu as pltpu
from jax.sharding import PartitionSpec as P


GROUPS = 32
TIME_TAPS = 5
TIME_DILATION = 2
BLOCKS = 2
LANES = 128
REACH = TIME_TAPS // 2

WHOLE = pl.BlockSpec(memory_space=pltpu.VMEM)
PLACED = pl.BlockSpec(memory_space=pl.ANY)
GRANT = 26 << 20


def lane_tile(index, tiles=1):
    return pl.ds(pl.multiple_of(index * LANES, LANES), tiles * LANES)


def float_tile(frame, index):
    return frame[:, lane_tile(index)].astype(jnp.float32)


def fold_groups(total, width):
    per_group = width // GROUPS
    total = jnp.broadcast_to(jnp.sum(total, axis=0, keepdims=True), total.shape)
    total = total + pltpu.roll(total, width, 1)
    lane = lax.broadcasted_iota(jnp.int32, total.shape, 1)
    step = 1
    while step < per_group:
        ahead, behind = pltpu.roll(total, LANES - step, 1), pltpu.roll(total, step, 1)
        total = total + jnp.where((lane // step) % 2 == 0, ahead, behind)
        step *= 2
    return total[:1]


def by_sublane(values):
    return jnp.sum(values.reshape(-1, 8, LANES), axis=0)


def summed(frame, tiles, width):
    pivot = pivot_of(float_tile(frame, 0), width)
    zero = jnp.zeros((8, LANES), jnp.float32)

    def gather(index, totals):
        return gathered(float_tile(frame, index), pivot, totals)

    return (pivot, *lax.fori_loop(0, tiles, gather, (zero, zero), unroll=16))


def pivot_of(tile, width):
    return fold_groups(by_sublane(tile), width) / (tile.shape[0] * LANES // GROUPS)


def gathered(tile, pivot, totals):
    shifted = tile - pivot
    return totals[0] + by_sublane(shifted), totals[1] + by_sublane(shifted * shifted)


def scaling(sums, gain, entries, width):
    pivot, first, second = sums
    offset = fold_groups(first, width) / entries
    spread = fold_groups(second, width) / entries - offset * offset
    scale = lax.rsqrt(jnp.maximum(spread, 0.0) + 1e-06)
    return pivot + offset, scale * jnp.concatenate([gain] * (LANES // width), 1) * 0.5


def convolve(stages, bands, gain, tiles, width):
    height = stages[0][2].shape[0]
    pack = tiles
    entries = height * tiles * LANES // GROUPS
    row = lax.broadcasted_iota(jnp.int32, (height, LANES), 0)
    lane = lax.broadcasted_iota(jnp.int32, (height, LANES), 1)

    def activate(stage, first, last):
        frame, (mean, scale), act = stage
        for i in range(pack):
            at = lane_tile(first * pack + i)
            half = (frame[:, at].astype(jnp.float32) - mean) * scale
            turned = pltpu.roll(half + half * jnp.tanh(half), width, 1)
            act[:, at] = jnp.where(lane < width, last, turned).astype(jnp.bfloat16)
            last = turned
        return last

    def conv(act, result, first):
        rows = [act[:, lane_tile(first * pack + i, 2)] for i in range(pack)]
        total = jnp.dot(jnp.concatenate(rows, 0), bands, preferred_element_type=jnp.float32)
        for i in range(pack):
            part = total[i * height : (i + 1) * height]
            above = jnp.where(row == 0, 0.0, pltpu.roll(part[:, :LANES], 1, 0))
            below = pltpu.roll(part[:, 2 * LANES :], height - 1, 0)
            below = jnp.where(row == height - 1, 0.0, below)
            sums = above + part[:, LANES : 2 * LANES] + below
            result[:, lane_tile(first * pack + i)] = sums.astype(jnp.bfloat16)

    before = None
    for stage in [*stages, None]:
        now = None
        if stage is not None:
            frame, sums, result, act = stage
            now = frame, scaling(sums, gain, entries, width), act

        def block(first, last, now=now, before=before):
            if before is not None:
                conv(*before, first)
            return last if now is None else activate(now, first, last)

        last = lax.fori_loop(0, tiles // pack, block, jnp.zeros((height, LANES), jnp.float32))
        before = None
        if stage is not None:
            act[:, lane_tile(tiles)] = jnp.where(lane < width, last, 0.0).astype(jnp.bfloat16)
            before = act, result


def normed_conv(frame, act, bands, gain, result, tiles, width):
    convolve([(frame, summed(frame, tiles, width), result, act)], bands, gain, tiles, width)


def temporal(sources, weights, tiles, emit, carry=0):
    height = sources[0].shape[0]
    pack = tiles

    def block(first, carry):
        rows = [
            jnp.concatenate([source[:, lane_tile(first * pack + i)] for source in sources], 1)
            for i in range(pack)
        ]
        total = jnp.dot(jnp.concatenate(rows, 0), weights, preferred_element_type=jnp.float32)
        for i in range(pack):
            part = total[i * height : (i + 1) * height]
            sums = [part[:, at : at + LANES] for at in range(0, weights.shape[1], LANES)]
            carry = emit(carry, first, i, lane_tile(first * pack + i), sums)
        return carry

    return lax.fori_loop(0, tiles // pack, block, carry)


def rounded(start, update):
    update = update.astype(jnp.bfloat16).astype(jnp.float32)
    return (start.astype(jnp.float32) + update).astype(jnp.bfloat16)


def keep(sources, weights, results, tiles):
    def emit(carry, first, i, at, sums):
        for result, total in zip(results, sums):
            result[:, at] = total
        return carry

    temporal(sources, weights, tiles, emit)


def add_up(start, partial, sources, weights, result, tiles):
    def emit(carry, first, i, at, sums):
        result[:, at] = rounded(start[:, at], partial[:, at] + sums[0])
        return carry

    temporal(sources, weights, tiles, emit)


def mix(starts, partials, sources, weights, results, tiles, width):
    def emit(carry, first, i, at, sums):
        after = []
        for place, (pivot, *totals) in enumerate(carry):
            update = sums[place] if partials is None else sums[place] + partials[place][:, at]
            added = rounded(starts[place][:, at], update)
            results[place][:, at] = added
            added = added.astype(jnp.float32)
            if i == 0:
                pivot = jnp.where(first == 0, pivot_of(added, width), pivot)
            after.append((pivot, *gathered(added, pivot, totals)))
        return after

    zero = jnp.zeros((8, LANES), jnp.float32)
    carry = [(zero[:1], zero, zero) for _ in starts]
    return temporal(sources, weights, tiles, emit, carry)


def marked_weights(table, marks, target, places):
    rows = []
    for mark, place in zip(marks, places):
        same = (mark == target).astype(jnp.float32)
        rows.append((table[place].astype(jnp.float32) * same).astype(jnp.bfloat16))
    return jnp.concatenate(rows, 0)


def mark_of(frame, tiles):
    return frame[0:16, lane_tile(tiles)].astype(jnp.float32)[:1]


def fetch(source, target, sem):
    copy = pltpu.make_async_copy(source, target, sem)
    copy.start()
    copy.wait()


def mark_kernel(ids, frame, marked, sem):
    columns = frame.shape[-1]
    copy = pltpu.make_async_copy(frame.at[0], marked.at[:, pl.ds(0, columns)], sem)
    copy.start()
    mark = jnp.broadcast_to(ids[...].astype(jnp.float32), (marked.shape[0], LANES))
    marked[:, columns:] = mark.astype(jnp.bfloat16)
    copy.wait()


def mark_frames(frames, clip_ids):
    _, height, columns = frames.shape
    return pl.pallas_call(
        mark_kernel,
        out_shape=jax.ShapeDtypeStruct((height, columns + LANES), frames.dtype),
        in_specs=[WHOLE, PLACED],
        out_specs=WHOLE,
        scratch_shapes=[pltpu.SemaphoreType.DMA],
        compiler_params=pltpu.CompilerParams(vmem_limit_bytes=4 << 20),
        name="mark_frames",
    )(clip_ids[:, None], frames)


def build_bands(space, bands):
    width = space.shape[-1]
    blank = jnp.zeros((width, width), jnp.bfloat16)
    for block in range(BLOCKS):
        for r in range(3):
            for a in range(4):
                pair = [space[block, r, a - b] if 0 <= a - b <= 2 else blank for b in (0, 1)]
                at = pl.ds(a * width, width), pl.ds(r * LANES, LANES)
                bands[(block, *at)] = jnp.concatenate(pair, 1)


def build_table(time, table, near):
    width = time.shape[-1]
    blank = jnp.zeros((width, width), jnp.bfloat16)
    for block in range(BLOCKS):
        for entry in range(TIME_TAPS + 2):
            if 1 <= entry <= TIME_TAPS:
                tap = jnp.where(near, entry - 1, TIME_TAPS - entry)
                matrix = time[block, tap]
            else:
                matrix = blank
            upper = jnp.concatenate([matrix, blank], 1)
            lower = jnp.concatenate([blank, matrix], 1)
            table[block, entry] = jnp.concatenate([upper, lower], 0)


def act_scratch(height, columns):
    return [pltpu.VMEM((height, columns), jnp.bfloat16)]


def like(frame, lanes=0):
    return jax.ShapeDtypeStruct((frame.shape[0], frame.shape[1] + lanes), jnp.bfloat16)


def estimate(frames):
    return pl.CostEstimate(
        flops=frames * 1_000_000_000, bytes_accessed=frames * 4_000_000, transcendentals=0
    )


def own_kernel(dims, where, frame, gains, space, time, conv, given, bands, table, act):
    tiles, width = dims
    build_bands(space, bands)
    build_table(time, table, where[0] == 1)
    normed_conv(frame, act, bands[0], gains[0:1], conv, tiles, width)
    core = jnp.full((conv.shape[0] - 16, LANES), where[2].astype(jnp.float32))
    mark = jnp.concatenate([frame[0:16, lane_tile(tiles)], core.astype(jnp.bfloat16)], 0)
    conv[:, lane_tile(tiles)] = mark
    for index in range(tiles // 2):
        given[:, lane_tile(index)] = conv[:, lane_tile((1 - where[2]) * (tiles // 2) + index)]
    given[:, lane_tile(tiles // 2)] = mark


def own_call(where, frame, gains, space, time):
    height, columns = frame.shape
    width = space.shape[-1]
    tiles = columns // LANES - 1
    return pl.pallas_call(
        functools.partial(own_kernel, (tiles, width)),
        out_shape=(
            like(frame),
            like(frame, -(tiles // 2) * LANES),
            jax.ShapeDtypeStruct((BLOCKS, 4 * width, 3 * LANES), jnp.bfloat16),
            jax.ShapeDtypeStruct((BLOCKS, TIME_TAPS + 2, LANES, LANES), jnp.bfloat16),
        ),
        in_specs=[pl.BlockSpec(memory_space=pltpu.SMEM)] + [WHOLE] * 4,
        out_specs=(WHOLE,) * 4,
        scratch_shapes=act_scratch(height, columns),
        compiler_params=pltpu.CompilerParams(vmem_limit_bytes=GRANT),
        cost_estimate=estimate(1),
        name="own",
    )(where, frame, gains, space, time)


def next_kernel(dims, *refs):
    tiles, width = dims
    where, outer, inner, gains, bands, ss, given, xn, sn, xo, so, half, act, sem = refs
    middle = where[1] == 1

    def conv(result, frame):
        normed_conv(frame, act, bands[0], gains[0:1], result, tiles, width)
        result[:, lane_tile(tiles)] = frame[:, lane_tile(tiles)]

    @pl.when(jnp.logical_not(middle))
    def _():
        fetch(outer, xn, sem)
        so[...] = jnp.zeros(so.shape, so.dtype)
        near, core = where[0].astype(jnp.float32), where[2].astype(jnp.float32)
        differ = (mark_of(ss, tiles) != mark_of(given, tiles // 2)).astype(jnp.float32)
        line = differ * near + (1.0 - differ) * (1.0 - near)
        mine = jnp.broadcast_to(line, (ss.shape[0], LANES)) == core
        for index in range(tiles // 2 + 1):
            place = where[2] * (tiles // 2) + index if index < tiles // 2 else tiles
            kept = jnp.where(mine, float_tile(ss, place), float_tile(given, index))
            half[:, lane_tile(index)] = kept.astype(jnp.bfloat16)

    @pl.when(middle)
    def _():
        fetch(outer, xo, sem)
        conv(so, xo)
        fetch(inner, xn, sem)

    conv(sn, xn)


def next_call(where, outer, inner, gains, bands, ss, given):
    height, columns = outer.shape
    tiles, width = columns // LANES - 1, gains.shape[-1]
    return pl.pallas_call(
        functools.partial(next_kernel, (tiles, width)),
        out_shape=(like(outer),) * 4 + (like(given),),
        in_specs=[pl.BlockSpec(memory_space=pltpu.SMEM), PLACED, PLACED] + [WHOLE] * 4,
        out_specs=(WHOLE,) * 5,
        scratch_shapes=act_scratch(height, columns) + [pltpu.SemaphoreType.DMA],
        compiler_params=pltpu.CompilerParams(vmem_limit_bytes=GRANT),
        cost_estimate=estimate(2),
        name="next",
    )(where, outer, inner, gains, bands, ss, given)


def places(middle, target):
    one = middle.astype(jnp.int32)
    lie = [one, one + 1, one + 2, 3 - 3 * one]
    return [at - lie[target] + REACH + 1 for at in lie]


def clamped(entries):
    return [jnp.clip(entry, 0, TIME_TAPS + 1) for entry in entries]


def weights_of(table, marks, middle, targets, kept):
    def column(target):
        entries = clamped(places(middle, target))
        chosen = [marks[place] for place in kept], [entries[place] for place in kept]
        return marked_weights(table, chosen[0], marks[target], chosen[1])

    return jnp.concatenate([column(target) for target in targets], 1)


def after_kernel(dims, *refs):
    tiles, width = dims
    where, xa, gains, bands, table, xs, ss, sn, xo, so = refs[:10]
    sa, xs1, *partial = refs[10:15]
    act, act_too, x1, ss1, so1 = refs[15:]
    middle = where[1] == 1

    normed_conv(xa, act, bands[0], gains[0:1], sa, tiles, width)
    sa[:, lane_tile(tiles)] = xa[:, lane_tile(tiles)]

    sources = (ss, sn, sa, so)
    marks = [mark_of(source, tiles) for source in sources]
    weights = weights_of(table.at[0], marks, middle, (0, 3), (0, 1, 2, 3))
    sums_s, sums_o = mix((xs, xo), None, sources, weights, (xs1, x1), tiles, width)
    stages = [(xs1, sums_s, ss1, act), (x1, sums_o, so1, act_too)]

    @pl.when(jnp.logical_not(middle))
    def _():
        so1[...] = jnp.zeros(so1.shape, so1.dtype)
        convolve(stages[:1], bands[1], gains[1:2], tiles, width)

    pl.when(middle)(lambda: convolve(stages, bands[1], gains[1:2], tiles, width))

    weights = weights_of(table.at[1], marks, middle, (0,), (0, 3))
    keep((ss1, so1), weights, partial[:1], tiles)
    weights = weights_of(table.at[0], marks, middle, (1, 2), (0, 1, 2))
    keep((ss, sn, sa), weights, partial[1:], tiles)


def after_call(where, xa, gains, bands, table, xs, ss, sn, xo, so):
    height, columns = xs.shape
    tiles, width = columns // LANES - 1, gains.shape[-1]
    partial = jax.ShapeDtypeStruct((height, columns - LANES), jnp.float32)
    return pl.pallas_call(
        functools.partial(after_kernel, (tiles, width)),
        out_shape=(like(xs), like(xs), partial, partial, partial),
        in_specs=[pl.BlockSpec(memory_space=pltpu.SMEM)] + [WHOLE] * 9,
        out_specs=(WHOLE,) * 5,
        scratch_shapes=act_scratch(height, columns) * 5,
        compiler_params=pltpu.CompilerParams(vmem_limit_bytes=GRANT),
        cost_estimate=estimate(2),
        name="after",
    )(where, xa, gains, bands, table, xs, ss, sn, xo, so)


def last_kernel(dims, *refs):
    tiles, width = dims
    where, mine, given, gains, bands, table, ss, sn, so_mid, sa, xn, xa, xs1 = refs[:13]
    partial, out = refs[13:16], refs[16]
    act, act_too, so, xn1, xa1, sn1, sa1, sem = refs[17:]
    middle = where[1] == 1

    pl.when(middle)(lambda: fetch(so_mid, so, sem.at[0]))

    @pl.when(jnp.logical_not(middle))
    def _():
        part = tiles // 2
        copies = [
            (mine.at[:, lane_tile(0, part)], so.at[:, lane_tile(where[2] * part, part)]),
            (given.at[:, lane_tile(0, part)], so.at[:, lane_tile((1 - where[2]) * part, part)]),
            (mine.at[:, lane_tile(part)], so.at[:, lane_tile(tiles)]),
        ]
        copies = [pltpu.make_async_copy(*ends, sem.at[i]) for i, ends in enumerate(copies)]
        for copy in copies:
            copy.start()
        for copy in copies:
            copy.wait()

    sources = (ss, sn, sa, so)
    marks = [mark_of(source, tiles) for source in sources]
    core = so[16:32, lane_tile(tiles)].astype(jnp.float32)[:1]
    valid = jnp.logical_or(core == where[2].astype(jnp.float32), middle)
    marks[3] = jnp.where(valid, marks[3], -1.0)
    weights = weights_of(table.at[0], marks, middle, (1, 2), (3,))
    sums_n, sums_a = mix((xn, xa), partial[1:], (so,), weights, (xn1, xa1), tiles, width)
    stages = [(xn1, sums_n, sn1, act), (xa1, sums_a, sa1, act_too)]
    convolve(stages, bands[1], gains[1:2], tiles, width)

    weights = weights_of(table.at[1], marks, middle, (0,), (1, 2))
    add_up(xs1, partial[0], (sn1, sa1), weights, out.at[0], tiles)


def last_call(where, mine, given, gains, bands, table, ss, sn, so, sa, xn, xa, xs1, *partial):
    height, columns = ss.shape
    tiles, width = columns // LANES - 1, gains.shape[-1]
    return pl.pallas_call(
        functools.partial(last_kernel, (tiles, width)),
        out_shape=jax.ShapeDtypeStruct((1, height, columns - LANES), jnp.bfloat16),
        in_specs=[pl.BlockSpec(memory_space=pltpu.SMEM)] + [PLACED] * 2 + [WHOLE] * 13,
        out_specs=WHOLE,
        scratch_shapes=act_scratch(height, columns) * 7 + [pltpu.SemaphoreType.DMA((3,))],
        compiler_params=pltpu.CompilerParams(vmem_limit_bytes=GRANT),
        cost_estimate=estimate(3),
        name="last",
    )(where, mine, given, gains, bands, table, ss, sn, so, sa, xn, xa, xs1, *partial)


def moved(values, hops, swap=()):
    pairs = []
    for a, b in hops:
        for core in range(TIME_DILATION):
            target = TIME_DILATION - 1 - core if a in swap else core
            pairs.append((TIME_DILATION * a + core, TIME_DILATION * b + target))
    return lax.ppermute(values, "dev", pairs)


def on_a_line(frames, clip_ids, norm_gain, space_kernel, time_kernel):
    device = lax.axis_index("dev")
    chip = device // TIME_DILATION
    near, middle = chip < 2, (chip == 1) | (chip == 2)
    where = jnp.stack([near, middle, device % TIME_DILATION == 1]).astype(jnp.int32)
    xs = mark_frames(frames, clip_ids)
    inner = moved(xs, [(0, 0), (1, 2), (2, 1), (3, 3)])
    outer = moved(xs, [(0, 1), (1, 0), (2, 3), (3, 2)])
    ss, given, bands, table = own_call(where, xs, norm_gain, space_kernel, time_kernel)
    given = moved(given, [(chip, chip) for chip in range(4)], swap=range(4))
    outer, _ = lax.optimization_barrier((outer, given))
    inner, _ = lax.optimization_barrier((inner, outer))
    after = moved(inner, [(0, 2), (1, 0), (2, 3), (3, 1)])
    xn, sn, xo, so, half = next_call(where, outer, inner, norm_gain, bands, ss, given)
    mine = moved(half, [(0, 3), (1, 1), (2, 2), (3, 0)])
    sa, xs1, *partial = after_call(
        where, after, norm_gain, bands, table, xs, ss, sn, xo, so
    )
    mine, _ = lax.optimization_barrier((mine, sa))
    given = moved(mine, [(chip, chip) for chip in range(4)], swap=range(4))
    return last_call(
        where, mine, given, norm_gain, bands, table, ss, sn, so, sa, xn, after, xs1, *partial
    )


def conv_kernel(dims, block, frame, gains, bands, conv, act):
    tiles, width = dims
    normed_conv(frame, act, bands[block], gains[block : block + 1], conv, tiles, width)
    conv[:, lane_tile(tiles)] = frame[:, lane_tile(tiles)]


def conv_call(block, frame, gains, bands):
    height, columns = frame.shape
    tiles, width = columns // LANES - 1, gains.shape[-1]
    return pl.pallas_call(
        functools.partial(conv_kernel, (tiles, width), block),
        out_shape=like(frame),
        in_specs=[WHOLE] * 3,
        out_specs=WHOLE,
        scratch_shapes=act_scratch(height, columns),
        compiler_params=pltpu.CompilerParams(vmem_limit_bytes=GRANT),
        name="conv",
    )(frame, gains, bands)


def mix_kernel(dims, block, frame, table, *refs):
    tiles, width = dims
    sources, result = refs[:TIME_TAPS], refs[TIME_TAPS]
    marks = [mark_of(source, tiles) for source in sources]
    entries = range(1, TIME_TAPS + 1)
    weights = marked_weights(table.at[block], marks, marks[REACH], entries)
    mix([frame], None, sources, weights, [result], tiles, width)
    result[:, lane_tile(tiles)] = frame[:, lane_tile(tiles)]


def mix_call(block, frame, table, sources, width):
    return pl.pallas_call(
        functools.partial(mix_kernel, (frame.shape[1] // LANES - 1, width), block),
        out_shape=like(frame),
        in_specs=[WHOLE] * (2 + TIME_TAPS),
        out_specs=WHOLE,
        compiler_params=pltpu.CompilerParams(vmem_limit_bytes=GRANT),
        name="mix",
    )(frame, table, *sources)


def by_relays(frames, clip_ids, norm_gain, space_kernel, time_kernel):
    chips = lax.axis_size("dev") // TIME_DILATION
    up = [(i, i + 1) for i in range(chips - 1)]
    down = [(i + 1, i) for i in range(chips - 1)]
    frame = mark_frames(frames, clip_ids)
    where = jnp.array([1, 0, 0], jnp.int32)
    conv, _, bands, table = own_call(where, frame, norm_gain, space_kernel, time_kernel)
    for block in range(BLOCKS):
        if block > 0:
            conv = conv_call(block, frame, norm_gain, bands)
        sources = [conv]
        for _ in range(REACH):
            sources = [moved(sources[0], up)] + sources + [moved(sources[-1], down)]
        frame = mix_call(block, frame, table, sources, norm_gain.shape[-1])
    return frame[None, :, : frames.shape[2]]


def per_device(*args):
    return (on_a_line if lax.axis_size("dev") == 8 else by_relays)(*args)


def solution(mesh):
    return jax.shard_map(
        per_device,
        mesh=mesh,
        in_specs=(P(("dp", "dev"), None, None), P(("dp", "dev")), P(), P(), P()),
        out_specs=P(("dp", "dev"), None, None),
        check_vma=False,
    )
```

```python
import functools

import jax
import jax.numpy as jnp
from jax import lax
from jax.experimental import pallas as pl
from jax.experimental.pallas import tpu as pltpu
from jax.sharding import PartitionSpec as P


GROUPS = 32
TIME_TAPS = 5
TIME_DILATION = 2
BLOCKS = 2
LANES = 128
REACH = TIME_TAPS // 2

WHOLE = pl.BlockSpec(memory_space=pltpu.VMEM)
PLACED = pl.BlockSpec(memory_space=pl.ANY)
GRANT = 26 << 20


def lane_tile(index, tiles=1):
    return pl.ds(pl.multiple_of(index * LANES, LANES), tiles * LANES)


def float_tile(frame, index):
    return frame[:, lane_tile(index)].astype(jnp.float32)


def fold_groups(total, width):
    per_group = width // GROUPS
    total = jnp.broadcast_to(jnp.sum(total, axis=0, keepdims=True), total.shape)
    total = total + pltpu.roll(total, width, 1)
    lane = lax.broadcasted_iota(jnp.int32, total.shape, 1)
    step = 1
    while step < per_group:
        ahead, behind = pltpu.roll(total, LANES - step, 1), pltpu.roll(total, step, 1)
        total = total + jnp.where((lane // step) % 2 == 0, ahead, behind)
        step *= 2
    return total[:1]


def by_sublane(values):
    return jnp.sum(values.reshape(-1, 8, LANES), axis=0)


def summed(frame, tiles, width):
    pivot = pivot_of(float_tile(frame, 0), width)
    zero = jnp.zeros((8, LANES), jnp.float32)

    def gather(index, totals):
        return gathered(float_tile(frame, index), pivot, totals)

    return (pivot, *lax.fori_loop(0, tiles, gather, (zero, zero), unroll=16))


def pivot_of(tile, width):
    return fold_groups(by_sublane(tile), width) / (tile.shape[0] * LANES // GROUPS)


def gathered(tile, pivot, totals):
    shifted = tile - pivot
    return totals[0] + by_sublane(shifted), totals[1] + by_sublane(shifted * shifted)


def scaling(sums, gain, entries, width):
    pivot, first, second = sums
    offset = fold_groups(first, width) / entries
    spread = fold_groups(second, width) / entries - offset * offset
    scale = lax.rsqrt(jnp.maximum(spread, 0.0) + 1e-06)
    return pivot + offset, scale * jnp.concatenate([gain] * (LANES // width), 1) * 0.5


def convolve(stages, bands, gain, tiles, width):
    height = stages[0][2].shape[0]
    entries = height * tiles * LANES // GROUPS
    row = lax.broadcasted_iota(jnp.int32, (height, LANES), 0)
    lane = lax.broadcasted_iota(jnp.int32, (height, LANES), 1)

    def activate(frame, scaled, act):
        mean, scale = scaled
        last = jnp.zeros((height, LANES), jnp.float32)
        for i in range(tiles):
            at = lane_tile(i)
            half = (frame[:, at].astype(jnp.float32) - mean) * scale
            turned = pltpu.roll(half + half * jnp.tanh(half), width, 1)
            act[:, at] = jnp.where(lane < width, last, turned).astype(jnp.bfloat16)
            last = turned
        act[:, lane_tile(tiles)] = jnp.where(lane < width, last, 0.0).astype(jnp.bfloat16)

    def conv(act, result):
        rows = [act[:, lane_tile(i, 2)] for i in range(tiles)]
        total = jnp.dot(jnp.concatenate(rows, 0), bands, preferred_element_type=jnp.float32)
        for i in range(tiles):
            part = total[i * height : (i + 1) * height]
            above = jnp.where(row == 0, 0.0, pltpu.roll(part[:, :LANES], 1, 0))
            below = pltpu.roll(part[:, 2 * LANES :], height - 1, 0)
            below = jnp.where(row == height - 1, 0.0, below)
            sums = above + part[:, LANES : 2 * LANES] + below
            result[:, lane_tile(i)] = sums.astype(jnp.bfloat16)

    before = None
    for frame, sums, result, act in stages:
        scaled = scaling(sums, gain, entries, width)
        if before is not None:
            conv(*before)
        activate(frame, scaled, act)
        before = act, result
    conv(*before)


def normed_conv(frame, act, bands, gain, result, tiles, width):
    convolve([(frame, summed(frame, tiles, width), result, act)], bands, gain, tiles, width)


def temporal(sources, weights, tiles, emit, carry=0):
    height = sources[0].shape[0]
    rows = [
        jnp.concatenate([source[:, lane_tile(i)] for source in sources], 1) for i in range(tiles)
    ]
    total = jnp.dot(jnp.concatenate(rows, 0), weights, preferred_element_type=jnp.float32)
    for i in range(tiles):
        part = total[i * height : (i + 1) * height]
        sums = [part[:, at : at + LANES] for at in range(0, weights.shape[1], LANES)]
        carry = emit(carry, i, sums)
    return carry


def rounded(start, update):
    update = update.astype(jnp.bfloat16).astype(jnp.float32)
    return (start.astype(jnp.float32) + update).astype(jnp.bfloat16)


def keep(sources, weights, results, tiles):
    def emit(carry, i, sums):
        at = lane_tile(i)
        for result, total in zip(results, sums):
            result[:, at] = total
        return carry

    temporal(sources, weights, tiles, emit)


def add_up(start, partial, sources, weights, held, result, sems, tiles):
    part = tiles // 4
    copies = []

    def emit(carry, i, sums):
        at = lane_tile(i)
        held[:, at] = rounded(start[:, at], partial[:, at] + sums[0])
        if i % part == part - 1:
            columns = pl.ds((i + 1 - part) * LANES, part * LANES)
            copy = held.at[:, columns], result.at[:, columns], sems.at[i // part]
            copies.append(pltpu.make_async_copy(*copy))
            copies[-1].start()
        return carry

    temporal(sources, weights, tiles, emit)
    for copy in copies:
        copy.wait()


def mix(starts, partials, sources, weights, results, tiles, width):
    def emit(carry, i, sums):
        at = lane_tile(i)
        after = []
        for place, (pivot, *totals) in enumerate(carry):
            update = sums[place] if partials is None else sums[place] + partials[place][:, at]
            added = rounded(starts[place][:, at], update)
            results[place][:, at] = added
            added = added.astype(jnp.float32)
            if i == 0:
                pivot = pivot_of(added, width)
            after.append((pivot, *gathered(added, pivot, totals)))
        return after

    zero = jnp.zeros((8, LANES), jnp.float32)
    carry = [(zero[:1], zero, zero) for _ in starts]
    return temporal(sources, weights, tiles, emit, carry)


def marked_weights(table, marks, target, places):
    rows = []
    for mark, place in zip(marks, places):
        same = (mark == target).astype(jnp.float32)
        rows.append((table[place].astype(jnp.float32) * same).astype(jnp.bfloat16))
    return jnp.concatenate(rows, 0)


def mark_of(frame, tiles):
    return frame[0:16, lane_tile(tiles)].astype(jnp.float32)[:1]


def fetch(source, target, sem):
    copy = pltpu.make_async_copy(source, target, sem)
    copy.start()
    copy.wait()


def mark_kernel(ids, frame, marked, sem):
    columns = frame.shape[-1]
    copy = pltpu.make_async_copy(frame.at[0], marked.at[:, pl.ds(0, columns)], sem)
    copy.start()
    mark = jnp.broadcast_to(ids[...].astype(jnp.float32), (marked.shape[0], LANES))
    marked[:, columns:] = mark.astype(jnp.bfloat16)
    copy.wait()


def mark_frames(frames, clip_ids):
    _, height, columns = frames.shape
    return pl.pallas_call(
        mark_kernel,
        out_shape=jax.ShapeDtypeStruct((height, columns + LANES), frames.dtype),
        in_specs=[WHOLE, PLACED],
        out_specs=WHOLE,
        scratch_shapes=[pltpu.SemaphoreType.DMA],
        compiler_params=pltpu.CompilerParams(vmem_limit_bytes=4 << 20),
        name="mark_frames",
    )(clip_ids[:, None], frames)


def build_bands(space, bands):
    width = space.shape[-1]
    blank = jnp.zeros((width, width), jnp.bfloat16)
    for block in range(BLOCKS):
        for r in range(3):
            for a in range(4):
                pair = [space[block, r, a - b] if 0 <= a - b <= 2 else blank for b in (0, 1)]
                at = pl.ds(a * width, width), pl.ds(r * LANES, LANES)
                bands[(block, *at)] = jnp.concatenate(pair, 1)


def build_table(time, table, near):
    width = time.shape[-1]
    blank = jnp.zeros((width, width), jnp.bfloat16)
    for block in range(BLOCKS):
        for entry in range(TIME_TAPS + 2):
            if 1 <= entry <= TIME_TAPS:
                tap = jnp.where(near, entry - 1, TIME_TAPS - entry)
                matrix = time[block, tap]
            else:
                matrix = blank
            upper = jnp.concatenate([matrix, blank], 1)
            lower = jnp.concatenate([blank, matrix], 1)
            table[block, entry] = jnp.concatenate([upper, lower], 0)


def act_scratch(height, columns):
    return [pltpu.VMEM((height, columns), jnp.bfloat16)]


def like(frame, lanes=0):
    return jax.ShapeDtypeStruct((frame.shape[0], frame.shape[1] + lanes), jnp.bfloat16)


def estimate(frames):
    return pl.CostEstimate(
        flops=frames * 1_000_000_000, bytes_accessed=frames * 4_000_000, transcendentals=0
    )


def own_kernel(dims, where, frame, gains, space, time, conv, given, bands, table, act):
    tiles, width = dims
    build_bands(space, bands)
    build_table(time, table, where[0] == 1)
    normed_conv(frame, act, bands[0], gains[0:1], conv, tiles, width)
    core = jnp.full((conv.shape[0] - 16, LANES), where[2].astype(jnp.float32))
    mark = jnp.concatenate([frame[0:16, lane_tile(tiles)], core.astype(jnp.bfloat16)], 0)
    conv[:, lane_tile(tiles)] = mark
    for index in range(tiles // 2):
        given[:, lane_tile(index)] = conv[:, lane_tile((1 - where[2]) * (tiles // 2) + index)]
    given[:, lane_tile(tiles // 2)] = mark


def own_call(where, frame, gains, space, time):
    height, columns = frame.shape
    width = space.shape[-1]
    tiles = columns // LANES - 1
    return pl.pallas_call(
        functools.partial(own_kernel, (tiles, width)),
        out_shape=(
            like(frame),
            like(frame, -(tiles // 2) * LANES),
            jax.ShapeDtypeStruct((BLOCKS, 4 * width, 3 * LANES), jnp.bfloat16),
            jax.ShapeDtypeStruct((BLOCKS, TIME_TAPS + 2, LANES, LANES), jnp.bfloat16),
        ),
        in_specs=[pl.BlockSpec(memory_space=pltpu.SMEM)] + [WHOLE] * 4,
        out_specs=(WHOLE,) * 4,
        scratch_shapes=act_scratch(height, columns),
        compiler_params=pltpu.CompilerParams(vmem_limit_bytes=GRANT),
        cost_estimate=estimate(1),
        name="own",
    )(where, frame, gains, space, time)


def next_kernel(dims, *refs):
    tiles, width = dims
    where, outer, inner, gains, bands, ss, given, xn, sn, xo, so, half, act, sem = refs
    middle = where[1] == 1

    def conv(result, frame):
        normed_conv(frame, act, bands[0], gains[0:1], result, tiles, width)
        result[:, lane_tile(tiles)] = frame[:, lane_tile(tiles)]

    @pl.when(jnp.logical_not(middle))
    def _():
        fetch(outer, xn, sem)
        so[...] = jnp.zeros(so.shape, so.dtype)
        near, core = where[0].astype(jnp.float32), where[2].astype(jnp.float32)
        differ = (mark_of(ss, tiles) != mark_of(given, tiles // 2)).astype(jnp.float32)
        line = differ * near + (1.0 - differ) * (1.0 - near)
        mine = jnp.broadcast_to(line, (ss.shape[0], LANES)) == core
        for index in range(tiles // 2 + 1):
            place = where[2] * (tiles // 2) + index if index < tiles // 2 else tiles
            kept = jnp.where(mine, float_tile(ss, place), float_tile(given, index))
            half[:, lane_tile(index)] = kept.astype(jnp.bfloat16)

    @pl.when(middle)
    def _():
        fetch(outer, xo, sem)
        conv(so, xo)
        fetch(inner, xn, sem)

    conv(sn, xn)


def next_call(where, outer, inner, gains, bands, ss, given):
    height, columns = outer.shape
    tiles, width = columns // LANES - 1, gains.shape[-1]
    return pl.pallas_call(
        functools.partial(next_kernel, (tiles, width)),
        out_shape=(like(outer),) * 4 + (like(given),),
        in_specs=[pl.BlockSpec(memory_space=pltpu.SMEM), PLACED, PLACED] + [WHOLE] * 4,
        out_specs=(WHOLE,) * 5,
        scratch_shapes=act_scratch(height, columns) + [pltpu.SemaphoreType.DMA],
        compiler_params=pltpu.CompilerParams(vmem_limit_bytes=GRANT),
        cost_estimate=estimate(2),
        name="next",
    )(where, outer, inner, gains, bands, ss, given)


def places(middle, target):
    one = middle.astype(jnp.int32)
    lie = [one, one + 1, one + 2, 3 - 3 * one]
    return [at - lie[target] + REACH + 1 for at in lie]


def clamped(entries):
    return [jnp.clip(entry, 0, TIME_TAPS + 1) for entry in entries]


def weights_of(table, marks, middle, targets, kept):
    def column(target):
        entries = clamped(places(middle, target))
        chosen = [marks[place] for place in kept], [entries[place] for place in kept]
        return marked_weights(table, chosen[0], marks[target], chosen[1])

    return jnp.concatenate([column(target) for target in targets], 1)


def after_kernel(dims, *refs):
    tiles, width = dims
    where, xa, gains, bands, table, xs, ss, sn, xo, so = refs[:10]
    sa, xs1, *partial = refs[10:15]
    act, act_too, x1, ss1, so1 = refs[15:]
    middle = where[1] == 1

    normed_conv(xa, act, bands[0], gains[0:1], sa, tiles, width)
    sa[:, lane_tile(tiles)] = xa[:, lane_tile(tiles)]

    sources = (ss, sn, sa, so)
    marks = [mark_of(source, tiles) for source in sources]
    weights = weights_of(table.at[0], marks, middle, (0, 3), (0, 1, 2, 3))
    sums_s, sums_o = mix((xs, xo), None, sources, weights, (xs1, x1), tiles, width)
    stages = [(xs1, sums_s, ss1, act), (x1, sums_o, so1, act_too)]

    @pl.when(jnp.logical_not(middle))
    def _():
        so1[...] = jnp.zeros(so1.shape, so1.dtype)
        convolve(stages[:1], bands[1], gains[1:2], tiles, width)

    pl.when(middle)(lambda: convolve(stages, bands[1], gains[1:2], tiles, width))

    weights = weights_of(table.at[1], marks, middle, (0,), (0, 3))
    keep((ss1, so1), weights, partial[:1], tiles)
    weights = weights_of(table.at[0], marks, middle, (1, 2), (0, 1, 2))
    keep((ss, sn, sa), weights, partial[1:], tiles)


def after_call(where, xa, gains, bands, table, xs, ss, sn, xo, so):
    height, columns = xs.shape
    tiles, width = columns // LANES - 1, gains.shape[-1]
    partial = jax.ShapeDtypeStruct((height, columns - LANES), jnp.float32)
    return pl.pallas_call(
        functools.partial(after_kernel, (tiles, width)),
        out_shape=(like(xs), like(xs), partial, partial, partial),
        in_specs=[pl.BlockSpec(memory_space=pltpu.SMEM)] + [WHOLE] * 9,
        out_specs=(WHOLE,) * 5,
        scratch_shapes=act_scratch(height, columns) * 5,
        compiler_params=pltpu.CompilerParams(vmem_limit_bytes=GRANT),
        cost_estimate=estimate(2),
        name="after",
    )(where, xa, gains, bands, table, xs, ss, sn, xo, so)


def last_kernel(dims, *refs):
    tiles, width = dims
    where, mine, given, gains, bands, table, ss, sn, so_mid, sa, xn, xa, xs1 = refs[:13]
    partial, out = refs[13:16], refs[16]
    act, act_too, so, xn1, xa1, sn1, sa1, sem = refs[17:]
    middle = where[1] == 1

    pl.when(middle)(lambda: fetch(so_mid, so, sem.at[0]))

    @pl.when(jnp.logical_not(middle))
    def _():
        part = tiles // 2
        copies = [
            (mine.at[:, lane_tile(0, part)], so.at[:, lane_tile(where[2] * part, part)]),
            (given.at[:, lane_tile(0, part)], so.at[:, lane_tile((1 - where[2]) * part, part)]),
            (mine.at[:, lane_tile(part)], so.at[:, lane_tile(tiles)]),
        ]
        copies = [pltpu.make_async_copy(*ends, sem.at[i]) for i, ends in enumerate(copies)]
        for copy in copies:
            copy.start()
        for copy in copies:
            copy.wait()

    sources = (ss, sn, sa, so)
    marks = [mark_of(source, tiles) for source in sources]
    core = so[16:32, lane_tile(tiles)].astype(jnp.float32)[:1]
    valid = jnp.logical_or(core == where[2].astype(jnp.float32), middle)
    marks[3] = jnp.where(valid, marks[3], -1.0)
    weights = weights_of(table.at[0], marks, middle, (1, 2), (3,))
    sums_n, sums_a = mix((xn, xa), partial[1:], (so,), weights, (xn1, xa1), tiles, width)
    stages = [(xn1, sums_n, sn1, act), (xa1, sums_a, sa1, act_too)]
    convolve(stages, bands[1], gains[1:2], tiles, width)

    weights = weights_of(table.at[1], marks, middle, (0,), (1, 2))
    add_up(xs1, partial[0], (sn1, sa1), weights, act, out.at[0], sem, tiles)


def last_call(where, mine, given, gains, bands, table, ss, sn, so, sa, xn, xa, xs1, *partial):
    height, columns = ss.shape
    tiles, width = columns // LANES - 1, gains.shape[-1]
    return pl.pallas_call(
        functools.partial(last_kernel, (tiles, width)),
        out_shape=jax.ShapeDtypeStruct((1, height, columns - LANES), jnp.bfloat16),
        in_specs=[pl.BlockSpec(memory_space=pltpu.SMEM)] + [PLACED] * 2 + [WHOLE] * 13,
        out_specs=pl.BlockSpec(memory_space=pltpu.HBM),
        scratch_shapes=act_scratch(height, columns) * 7 + [pltpu.SemaphoreType.DMA((4,))],
        compiler_params=pltpu.CompilerParams(vmem_limit_bytes=GRANT),
        cost_estimate=estimate(3),
        name="last",
    )(where, mine, given, gains, bands, table, ss, sn, so, sa, xn, xa, xs1, *partial)


def moved(values, hops, swap=()):
    pairs = []
    for a, b in hops:
        for core in range(TIME_DILATION):
            target = TIME_DILATION - 1 - core if a in swap else core
            pairs.append((TIME_DILATION * a + core, TIME_DILATION * b + target))
    return lax.ppermute(values, "dev", pairs)


def on_a_line(frames, clip_ids, norm_gain, space_kernel, time_kernel):
    device = lax.axis_index("dev")
    chip = device // TIME_DILATION
    near, middle = chip < 2, (chip == 1) | (chip == 2)
    where = jnp.stack([near, middle, device % TIME_DILATION == 1]).astype(jnp.int32)
    xs = mark_frames(frames, clip_ids)
    inner = moved(xs, [(0, 0), (1, 2), (2, 1), (3, 3)])
    outer = moved(xs, [(0, 1), (1, 0), (2, 3), (3, 2)])
    ss, given, bands, table = own_call(where, xs, norm_gain, space_kernel, time_kernel)
    given = moved(given, [(chip, chip) for chip in range(4)], swap=range(4))
    outer, _ = lax.optimization_barrier((outer, given))
    inner, _ = lax.optimization_barrier((inner, given))
    after = moved(inner, [(0, 2), (1, 0), (2, 3), (3, 1)])
    xn, sn, xo, so, half = next_call(where, outer, inner, norm_gain, bands, ss, given)
    mine = moved(half, [(0, 3), (1, 1), (2, 2), (3, 0)])
    sa, xs1, *partial = after_call(
        where, after, norm_gain, bands, table, xs, ss, sn, xo, so
    )
    mine, _ = lax.optimization_barrier((mine, sa))
    given = moved(mine, [(chip, chip) for chip in range(4)], swap=range(4))
    return last_call(
        where, mine, given, norm_gain, bands, table, ss, sn, so, sa, xn, after, xs1, *partial
    )


def conv_kernel(dims, block, frame, gains, bands, conv, act):
    tiles, width = dims
    normed_conv(frame, act, bands[block], gains[block : block + 1], conv, tiles, width)
    conv[:, lane_tile(tiles)] = frame[:, lane_tile(tiles)]


def conv_call(block, frame, gains, bands):
    height, columns = frame.shape
    tiles, width = columns // LANES - 1, gains.shape[-1]
    return pl.pallas_call(
        functools.partial(conv_kernel, (tiles, width), block),
        out_shape=like(frame),
        in_specs=[WHOLE] * 3,
        out_specs=WHOLE,
        scratch_shapes=act_scratch(height, columns),
        compiler_params=pltpu.CompilerParams(vmem_limit_bytes=GRANT),
        name="conv",
    )(frame, gains, bands)


def mix_kernel(dims, block, frame, table, *refs):
    tiles, width = dims
    sources, result = refs[:TIME_TAPS], refs[TIME_TAPS]
    marks = [mark_of(source, tiles) for source in sources]
    entries = range(1, TIME_TAPS + 1)
    weights = marked_weights(table.at[block], marks, marks[REACH], entries)
    mix([frame], None, sources, weights, [result], tiles, width)
    result[:, lane_tile(tiles)] = frame[:, lane_tile(tiles)]


def mix_call(block, frame, table, sources, width):
    return pl.pallas_call(
        functools.partial(mix_kernel, (frame.shape[1] // LANES - 1, width), block),
        out_shape=like(frame),
        in_specs=[WHOLE] * (2 + TIME_TAPS),
        out_specs=WHOLE,
        compiler_params=pltpu.CompilerParams(vmem_limit_bytes=GRANT),
        name="mix",
    )(frame, table, *sources)


def by_relays(frames, clip_ids, norm_gain, space_kernel, time_kernel):
    chips = lax.axis_size("dev") // TIME_DILATION
    up = [(i, i + 1) for i in range(chips - 1)]
    down = [(i + 1, i) for i in range(chips - 1)]
    frame = mark_frames(frames, clip_ids)
    where = jnp.array([1, 0, 0], jnp.int32)
    conv, _, bands, table = own_call(where, frame, norm_gain, space_kernel, time_kernel)
    for block in range(BLOCKS):
        if block > 0:
            conv = conv_call(block, frame, norm_gain, bands)
        sources = [conv]
        for _ in range(REACH):
            sources = [moved(sources[0], up)] + sources + [moved(sources[-1], down)]
        frame = mix_call(block, frame, table, sources, norm_gain.shape[-1])
    return frame[None, :, : frames.shape[2]]


def per_device(*args):
    return (on_a_line if lax.axis_size("dev") == 8 else by_relays)(*args)


def solution(mesh):
    return jax.shard_map(
        per_device,
        mesh=mesh,
        in_specs=(P(("dp", "dev"), None, None), P(("dp", "dev")), P(), P(), P()),
        out_specs=P(("dp", "dev"), None, None),
        check_vma=False,
    )
```

```python
import functools

import jax
import jax.numpy as jnp
from jax import lax
from jax.experimental import pallas as pl
from jax.experimental.pallas import tpu as pltpu
from jax.sharding import PartitionSpec as P


GROUPS = 32
TIME_TAPS = 5
TIME_DILATION = 2
BLOCKS = 2
LANES = 128
REACH = TIME_TAPS // 2

WHOLE = pl.BlockSpec(memory_space=pltpu.VMEM)
PLACED = pl.BlockSpec(memory_space=pl.ANY)
GRANT = 26 << 20


def lane_tile(index, tiles=1):
    return pl.ds(pl.multiple_of(index * LANES, LANES), tiles * LANES)


def float_tile(frame, index):
    return frame[:, lane_tile(index)].astype(jnp.float32)


def fold_groups(total, width):
    per_group = width // GROUPS
    total = jnp.broadcast_to(jnp.sum(total, axis=0, keepdims=True), total.shape)
    total = total + pltpu.roll(total, width, 1)
    lane = lax.broadcasted_iota(jnp.int32, total.shape, 1)
    step = 1
    while step < per_group:
        ahead, behind = pltpu.roll(total, LANES - step, 1), pltpu.roll(total, step, 1)
        total = total + jnp.where((lane // step) % 2 == 0, ahead, behind)
        step *= 2
    return total[:1]


def by_sublane(values):
    return jnp.sum(values.reshape(-1, 8, LANES), axis=0)


def summed(frame, tiles, width):
    pivot = pivot_of(float_tile(frame, 0), width)
    zero = jnp.zeros((8, LANES), jnp.float32)

    def gather(index, totals):
        return gathered(float_tile(frame, index), pivot, totals)

    return (pivot, *lax.fori_loop(0, tiles, gather, (zero, zero), unroll=16))


def pivot_of(tile, width):
    return fold_groups(by_sublane(tile), width) / (tile.shape[0] * LANES // GROUPS)


def gathered(tile, pivot, totals):
    shifted = tile - pivot
    return totals[0] + by_sublane(shifted), totals[1] + by_sublane(shifted * shifted)


def scaling(sums, gain, entries, width):
    pivot, first, second = sums
    offset = fold_groups(first, width) / entries
    spread = fold_groups(second, width) / entries - offset * offset
    scale = lax.rsqrt(jnp.maximum(spread, 0.0) + 1e-06)
    return pivot + offset, scale * jnp.concatenate([gain] * (LANES // width), 1) * 0.5


def convolve(stages, bands, gain, tiles, width):
    height = stages[0][2].shape[0]
    entries = height * tiles * LANES // GROUPS
    row = lax.broadcasted_iota(jnp.int32, (height, LANES), 0)
    lane = lax.broadcasted_iota(jnp.int32, (height, LANES), 1)

    def activate(frame, scaled, act):
        mean, scale = scaled
        last = jnp.zeros((height, LANES), jnp.float32)
        for i in range(tiles):
            at = lane_tile(i)
            half = (frame[:, at].astype(jnp.float32) - mean) * scale
            turned = pltpu.roll(half + half * jnp.tanh(half), width, 1)
            act[:, at] = jnp.where(lane < width, last, turned).astype(jnp.bfloat16)
            last = turned
        act[:, lane_tile(tiles)] = jnp.where(lane < width, last, 0.0).astype(jnp.bfloat16)

    def conv(act, result):
        rows = [act[:, lane_tile(i, 2)] for i in range(tiles)]
        total = jnp.dot(jnp.concatenate(rows, 0), bands, preferred_element_type=jnp.float32)
        for i in range(tiles):
            part = total[i * height : (i + 1) * height]
            above = jnp.where(row == 0, 0.0, pltpu.roll(part[:, :LANES], 1, 0))
            below = pltpu.roll(part[:, 2 * LANES :], height - 1, 0)
            below = jnp.where(row == height - 1, 0.0, below)
            sums = above + part[:, LANES : 2 * LANES] + below
            result[:, lane_tile(i)] = sums.astype(jnp.bfloat16)

    before = None
    for frame, sums, result, act in stages:
        scaled = scaling(sums, gain, entries, width)
        if before is not None:
            conv(*before)
        activate(frame, scaled, act)
        before = act, result
    conv(*before)


def normed_conv(frame, act, bands, gain, result, tiles, width):
    convolve([(frame, summed(frame, tiles, width), result, act)], bands, gain, tiles, width)


def temporal(sources, weights, tiles, emit, carry=0):
    height = sources[0].shape[0]
    rows = [
        jnp.concatenate([source[:, lane_tile(i)] for source in sources], 1) for i in range(tiles)
    ]
    total = jnp.dot(jnp.concatenate(rows, 0), weights, preferred_element_type=jnp.float32)
    for i in range(tiles):
        part = total[i * height : (i + 1) * height]
        sums = [part[:, at : at + LANES] for at in range(0, weights.shape[1], LANES)]
        carry = emit(carry, i, sums)
    return carry


def rounded(start, update):
    update = update.astype(jnp.bfloat16).astype(jnp.float32)
    return (start.astype(jnp.float32) + update).astype(jnp.bfloat16)


def keep(sources, weights, results, tiles):
    def emit(carry, i, sums):
        at = lane_tile(i)
        for result, total in zip(results, sums):
            result[:, at] = total
        return carry

    temporal(sources, weights, tiles, emit)


def add_up(start, partial, sources, weights, held, result, sems, tiles):
    part = tiles // 4
    copies = []

    def emit(carry, i, sums):
        at = lane_tile(i)
        held[:, at] = rounded(start[:, at], partial[:, at] + sums[0])
        if i % part == part - 1:
            columns = pl.ds((i + 1 - part) * LANES, part * LANES)
            copy = held.at[:, columns], result.at[:, columns], sems.at[i // part]
            copies.append(pltpu.make_async_copy(*copy))
            copies[-1].start()
        return carry

    temporal(sources, weights, tiles, emit)
    for copy in copies:
        copy.wait()


def mix(starts, partials, sources, weights, results, tiles, width):
    def emit(carry, i, sums):
        at = lane_tile(i)
        after = []
        for place, (pivot, *totals) in enumerate(carry):
            update = sums[place] if partials is None else sums[place] + partials[place][:, at]
            added = rounded(starts[place][:, at], update)
            results[place][:, at] = added
            added = added.astype(jnp.float32)
            if i == 0:
                pivot = pivot_of(added, width)
            after.append((pivot, *gathered(added, pivot, totals)))
        return after

    zero = jnp.zeros((8, LANES), jnp.float32)
    carry = [(zero[:1], zero, zero) for _ in starts]
    return temporal(sources, weights, tiles, emit, carry)


def marked_weights(table, marks, target, places):
    rows = []
    for mark, place in zip(marks, places):
        same = (mark == target).astype(jnp.float32)
        rows.append((table[place].astype(jnp.float32) * same).astype(jnp.bfloat16))
    return jnp.concatenate(rows, 0)


def mark_of(frame, tiles):
    return frame[0:16, lane_tile(tiles)].astype(jnp.float32)[:1]


def fetch(source, target, sem):
    copy = pltpu.make_async_copy(source, target, sem)
    copy.start()
    copy.wait()


def mark_kernel(ids, frame, marked, held, sem, id_sem):
    columns = frame.shape[-1]
    id_copy = pltpu.make_async_copy(ids, held, id_sem)
    id_copy.start()
    copy = pltpu.make_async_copy(frame.at[0], marked.at[:, pl.ds(0, columns)], sem)
    copy.start()
    id_copy.wait()
    mark = jnp.full((marked.shape[0], LANES), held[0].astype(jnp.float32))
    marked[:, columns:] = mark.astype(jnp.bfloat16)
    copy.wait()


def mark_frames(frames, clip_ids):
    _, height, columns = frames.shape
    return pl.pallas_call(
        mark_kernel,
        out_shape=jax.ShapeDtypeStruct((height, columns + LANES), frames.dtype),
        in_specs=[pl.BlockSpec(memory_space=pltpu.HBM), PLACED],
        out_specs=WHOLE,
        scratch_shapes=[pltpu.SMEM((1,), jnp.int32)] + [pltpu.SemaphoreType.DMA] * 2,
        compiler_params=pltpu.CompilerParams(vmem_limit_bytes=4 << 20),
        name="mark_frames",
    )(clip_ids, frames)


def build_bands(space, bands):
    width = space.shape[-1]
    blank = jnp.zeros((width, width), jnp.bfloat16)
    for block in range(BLOCKS):
        for r in range(3):
            for a in range(4):
                pair = [space[block, r, a - b] if 0 <= a - b <= 2 else blank for b in (0, 1)]
                at = pl.ds(a * width, width), pl.ds(r * LANES, LANES)
                bands[(block, *at)] = jnp.concatenate(pair, 1)


def build_table(time, table, near):
    width = time.shape[-1]
    blank = jnp.zeros((width, width), jnp.bfloat16)
    for block in range(BLOCKS):
        for entry in range(TIME_TAPS + 2):
            if 1 <= entry <= TIME_TAPS:
                tap = jnp.where(near, entry - 1, TIME_TAPS - entry)
                matrix = time[block, tap]
            else:
                matrix = blank
            upper = jnp.concatenate([matrix, blank], 1)
            lower = jnp.concatenate([blank, matrix], 1)
            table[block, entry] = jnp.concatenate([upper, lower], 0)


def act_scratch(height, columns):
    return [pltpu.VMEM((height, columns), jnp.bfloat16)]


def like(frame, lanes=0):
    return jax.ShapeDtypeStruct((frame.shape[0], frame.shape[1] + lanes), jnp.bfloat16)


def estimate(frames):
    return pl.CostEstimate(
        flops=frames * 1_000_000_000, bytes_accessed=frames * 4_000_000, transcendentals=0
    )


def own_kernel(dims, where, frame, gains, space, time, conv, given, bands, table, act):
    tiles, width = dims
    build_bands(space, bands)
    build_table(time, table, where[0] == 1)
    normed_conv(frame, act, bands[0], gains[0:1], conv, tiles, width)
    core = jnp.full((conv.shape[0] - 16, LANES), where[2].astype(jnp.float32))
    mark = jnp.concatenate([frame[0:16, lane_tile(tiles)], core.astype(jnp.bfloat16)], 0)
    conv[:, lane_tile(tiles)] = mark
    for index in range(tiles // 2):
        given[:, lane_tile(index)] = conv[:, lane_tile((1 - where[2]) * (tiles // 2) + index)]
    given[:, lane_tile(tiles // 2)] = mark


def own_call(where, frame, gains, space, time):
    height, columns = frame.shape
    width = space.shape[-1]
    tiles = columns // LANES - 1
    return pl.pallas_call(
        functools.partial(own_kernel, (tiles, width)),
        out_shape=(
            like(frame),
            like(frame, -(tiles // 2) * LANES),
            jax.ShapeDtypeStruct((BLOCKS, 4 * width, 3 * LANES), jnp.bfloat16),
            jax.ShapeDtypeStruct((BLOCKS, TIME_TAPS + 2, LANES, LANES), jnp.bfloat16),
        ),
        in_specs=[pl.BlockSpec(memory_space=pltpu.SMEM)] + [WHOLE] * 4,
        out_specs=(WHOLE,) * 4,
        scratch_shapes=act_scratch(height, columns),
        compiler_params=pltpu.CompilerParams(vmem_limit_bytes=GRANT),
        cost_estimate=estimate(1),
        name="own",
    )(where, frame, gains, space, time)


def next_kernel(dims, *refs):
    tiles, width = dims
    where, outer, inner, gains, bands, ss, given, xn, sn, xo, so, half, act, sem = refs
    middle = where[1] == 1

    def conv(result, frame):
        normed_conv(frame, act, bands[0], gains[0:1], result, tiles, width)
        result[:, lane_tile(tiles)] = frame[:, lane_tile(tiles)]

    @pl.when(jnp.logical_not(middle))
    def _():
        fetch(outer, xn, sem)
        so[...] = jnp.zeros(so.shape, so.dtype)
        near, core = where[0].astype(jnp.float32), where[2].astype(jnp.float32)
        differ = (mark_of(ss, tiles) != mark_of(given, tiles // 2)).astype(jnp.float32)
        line = differ * near + (1.0 - differ) * (1.0 - near)
        mine = jnp.broadcast_to(line, (ss.shape[0], LANES)) == core
        for index in range(tiles // 2 + 1):
            place = where[2] * (tiles // 2) + index if index < tiles // 2 else tiles
            kept = jnp.where(mine, float_tile(ss, place), float_tile(given, index))
            half[:, lane_tile(index)] = kept.astype(jnp.bfloat16)

    @pl.when(middle)
    def _():
        fetch(outer, xo, sem)
        conv(so, xo)
        fetch(inner, xn, sem)

    conv(sn, xn)


def next_call(where, outer, inner, gains, bands, ss, given):
    height, columns = outer.shape
    tiles, width = columns // LANES - 1, gains.shape[-1]
    return pl.pallas_call(
        functools.partial(next_kernel, (tiles, width)),
        out_shape=(like(outer),) * 4 + (like(given),),
        in_specs=[pl.BlockSpec(memory_space=pltpu.SMEM), PLACED, PLACED] + [WHOLE] * 4,
        out_specs=(WHOLE,) * 5,
        scratch_shapes=act_scratch(height, columns) + [pltpu.SemaphoreType.DMA],
        compiler_params=pltpu.CompilerParams(vmem_limit_bytes=GRANT),
        cost_estimate=estimate(2),
        name="next",
    )(where, outer, inner, gains, bands, ss, given)


def places(middle, target):
    one = middle.astype(jnp.int32)
    lie = [one, one + 1, one + 2, 3 - 3 * one]
    return [at - lie[target] + REACH + 1 for at in lie]


def clamped(entries):
    return [jnp.clip(entry, 0, TIME_TAPS + 1) for entry in entries]


def weights_of(table, marks, middle, targets, kept):
    def column(target):
        entries = clamped(places(middle, target))
        chosen = [marks[place] for place in kept], [entries[place] for place in kept]
        return marked_weights(table, chosen[0], marks[target], chosen[1])

    return jnp.concatenate([column(target) for target in targets], 1)


def after_kernel(dims, *refs):
    tiles, width = dims
    where, xa, gains, bands, table, xs, ss, sn, xo, so = refs[:10]
    sa, xs1, *partial = refs[10:15]
    act, act_too, x1, ss1, so1 = refs[15:]
    middle = where[1] == 1

    normed_conv(xa, act, bands[0], gains[0:1], sa, tiles, width)
    sa[:, lane_tile(tiles)] = xa[:, lane_tile(tiles)]

    sources = (ss, sn, sa, so)
    marks = [mark_of(source, tiles) for source in sources]
    weights = weights_of(table.at[0], marks, middle, (0, 3), (0, 1, 2, 3))
    sums_s, sums_o = mix((xs, xo), None, sources, weights, (xs1, x1), tiles, width)
    stages = [(xs1, sums_s, ss1, act), (x1, sums_o, so1, act_too)]

    @pl.when(jnp.logical_not(middle))
    def _():
        so1[...] = jnp.zeros(so1.shape, so1.dtype)
        convolve(stages[:1], bands[1], gains[1:2], tiles, width)

    pl.when(middle)(lambda: convolve(stages, bands[1], gains[1:2], tiles, width))

    weights = weights_of(table.at[1], marks, middle, (0,), (0, 3))
    keep((ss1, so1), weights, partial[:1], tiles)
    weights = weights_of(table.at[0], marks, middle, (1, 2), (0, 1, 2))
    keep((ss, sn, sa), weights, partial[1:], tiles)


def after_call(where, xa, gains, bands, table, xs, ss, sn, xo, so):
    height, columns = xs.shape
    tiles, width = columns // LANES - 1, gains.shape[-1]
    partial = jax.ShapeDtypeStruct((height, columns - LANES), jnp.float32)
    return pl.pallas_call(
        functools.partial(after_kernel, (tiles, width)),
        out_shape=(like(xs), like(xs), partial, partial, partial),
        in_specs=[pl.BlockSpec(memory_space=pltpu.SMEM)] + [WHOLE] * 9,
        out_specs=(WHOLE,) * 5,
        scratch_shapes=act_scratch(height, columns) * 5,
        compiler_params=pltpu.CompilerParams(vmem_limit_bytes=GRANT),
        cost_estimate=estimate(2),
        name="after",
    )(where, xa, gains, bands, table, xs, ss, sn, xo, so)


def last_kernel(dims, *refs):
    tiles, width = dims
    where, mine, given, gains, bands, table, ss, sn, so_mid, sa, xn, xa, xs1 = refs[:13]
    partial, out = refs[13:16], refs[16]
    act, act_too, so, xn1, xa1, sn1, sa1, sem = refs[17:]
    middle = where[1] == 1

    pl.when(middle)(lambda: fetch(so_mid, so, sem.at[0]))

    @pl.when(jnp.logical_not(middle))
    def _():
        part = tiles // 2
        copies = [
            (mine.at[:, lane_tile(0, part)], so.at[:, lane_tile(where[2] * part, part)]),
            (given.at[:, lane_tile(0, part)], so.at[:, lane_tile((1 - where[2]) * part, part)]),
            (mine.at[:, lane_tile(part)], so.at[:, lane_tile(tiles)]),
        ]
        copies = [pltpu.make_async_copy(*ends, sem.at[i]) for i, ends in enumerate(copies)]
        for copy in copies:
            copy.start()
        for copy in copies:
            copy.wait()

    sources = (ss, sn, sa, so)
    marks = [mark_of(source, tiles) for source in sources]
    core = so[16:32, lane_tile(tiles)].astype(jnp.float32)[:1]
    valid = jnp.logical_or(core == where[2].astype(jnp.float32), middle)
    marks[3] = jnp.where(valid, marks[3], -1.0)
    weights = weights_of(table.at[0], marks, middle, (1, 2), (3,))
    sums_n, sums_a = mix((xn, xa), partial[1:], (so,), weights, (xn1, xa1), tiles, width)
    stages = [(xn1, sums_n, sn1, act), (xa1, sums_a, sa1, act_too)]
    convolve(stages, bands[1], gains[1:2], tiles, width)

    weights = weights_of(table.at[1], marks, middle, (0,), (1, 2))
    add_up(xs1, partial[0], (sn1, sa1), weights, act, out.at[0], sem, tiles)


def last_call(where, mine, given, gains, bands, table, ss, sn, so, sa, xn, xa, xs1, *partial):
    height, columns = ss.shape
    tiles, width = columns // LANES - 1, gains.shape[-1]
    return pl.pallas_call(
        functools.partial(last_kernel, (tiles, width)),
        out_shape=jax.ShapeDtypeStruct((1, height, columns - LANES), jnp.bfloat16),
        in_specs=[pl.BlockSpec(memory_space=pltpu.SMEM)] + [PLACED] * 2 + [WHOLE] * 13,
        out_specs=pl.BlockSpec(memory_space=pltpu.HBM),
        scratch_shapes=act_scratch(height, columns) * 7 + [pltpu.SemaphoreType.DMA((4,))],
        compiler_params=pltpu.CompilerParams(vmem_limit_bytes=GRANT),
        cost_estimate=estimate(3),
        name="last",
    )(where, mine, given, gains, bands, table, ss, sn, so, sa, xn, xa, xs1, *partial)


def moved(values, hops, swap=()):
    pairs = []
    for a, b in hops:
        for core in range(TIME_DILATION):
            target = TIME_DILATION - 1 - core if a in swap else core
            pairs.append((TIME_DILATION * a + core, TIME_DILATION * b + target))
    return lax.ppermute(values, "dev", pairs)


def on_a_line(frames, clip_ids, norm_gain, space_kernel, time_kernel):
    device = lax.axis_index("dev")
    chip = device // TIME_DILATION
    near, middle = chip < 2, (chip == 1) | (chip == 2)
    where = jnp.stack([near, middle, device % TIME_DILATION == 1]).astype(jnp.int32)
    xs = mark_frames(frames, clip_ids)
    inner = moved(xs, [(0, 0), (1, 2), (2, 1), (3, 3)])
    outer = moved(xs, [(0, 1), (1, 0), (2, 3), (3, 2)])
    ss, given, bands, table = own_call(where, xs, norm_gain, space_kernel, time_kernel)
    given = moved(given, [(chip, chip) for chip in range(4)], swap=range(4))
    outer, _ = lax.optimization_barrier((outer, given))
    inner, _ = lax.optimization_barrier((inner, given))
    after = moved(inner, [(0, 2), (1, 0), (2, 3), (3, 1)])
    xn, sn, xo, so, half = next_call(where, outer, inner, norm_gain, bands, ss, given)
    mine = moved(half, [(0, 3), (1, 1), (2, 2), (3, 0)])
    sa, xs1, *partial = after_call(
        where, after, norm_gain, bands, table, xs, ss, sn, xo, so
    )
    mine, _ = lax.optimization_barrier((mine, sa))
    given = moved(mine, [(chip, chip) for chip in range(4)], swap=range(4))
    return last_call(
        where, mine, given, norm_gain, bands, table, ss, sn, so, sa, xn, after, xs1, *partial
    )


def conv_kernel(dims, block, frame, gains, bands, conv, act):
    tiles, width = dims
    normed_conv(frame, act, bands[block], gains[block : block + 1], conv, tiles, width)
    conv[:, lane_tile(tiles)] = frame[:, lane_tile(tiles)]


def conv_call(block, frame, gains, bands):
    height, columns = frame.shape
    tiles, width = columns // LANES - 1, gains.shape[-1]
    return pl.pallas_call(
        functools.partial(conv_kernel, (tiles, width), block),
        out_shape=like(frame),
        in_specs=[WHOLE] * 3,
        out_specs=WHOLE,
        scratch_shapes=act_scratch(height, columns),
        compiler_params=pltpu.CompilerParams(vmem_limit_bytes=GRANT),
        name="conv",
    )(frame, gains, bands)


def mix_kernel(dims, block, frame, table, *refs):
    tiles, width = dims
    sources, result = refs[:TIME_TAPS], refs[TIME_TAPS]
    marks = [mark_of(source, tiles) for source in sources]
    entries = range(1, TIME_TAPS + 1)
    weights = marked_weights(table.at[block], marks, marks[REACH], entries)
    mix([frame], None, sources, weights, [result], tiles, width)
    result[:, lane_tile(tiles)] = frame[:, lane_tile(tiles)]


def mix_call(block, frame, table, sources, width):
    return pl.pallas_call(
        functools.partial(mix_kernel, (frame.shape[1] // LANES - 1, width), block),
        out_shape=like(frame),
        in_specs=[WHOLE] * (2 + TIME_TAPS),
        out_specs=WHOLE,
        compiler_params=pltpu.CompilerParams(vmem_limit_bytes=GRANT),
        name="mix",
    )(frame, table, *sources)


def by_relays(frames, clip_ids, norm_gain, space_kernel, time_kernel):
    chips = lax.axis_size("dev") // TIME_DILATION
    up = [(i, i + 1) for i in range(chips - 1)]
    down = [(i + 1, i) for i in range(chips - 1)]
    frame = mark_frames(frames, clip_ids)
    where = jnp.array([1, 0, 0], jnp.int32)
    conv, _, bands, table = own_call(where, frame, norm_gain, space_kernel, time_kernel)
    for block in range(BLOCKS):
        if block > 0:
            conv = conv_call(block, frame, norm_gain, bands)
        sources = [conv]
        for _ in range(REACH):
            sources = [moved(sources[0], up)] + sources + [moved(sources[-1], down)]
        frame = mix_call(block, frame, table, sources, norm_gain.shape[-1])
    return frame[None, :, : frames.shape[2]]


def per_device(*args):
    return (on_a_line if lax.axis_size("dev") == 8 else by_relays)(*args)


def solution(mesh):
    return jax.shard_map(
        per_device,
        mesh=mesh,
        in_specs=(P(("dp", "dev"), None, None), P(("dp", "dev")), P(), P(), P()),
        out_specs=P(("dp", "dev"), None, None),
        check_vma=False,
    )
```
